32 devices in a mesh: groups: 2 (over x), row: 16 (over z, y, core).
Axes of the slice: x: 2, y: 2, z: 4, core: 2. Of those that a mesh axis runs over, the one named last changes fastest.
Arguments:
- homolog_embedding: bfloat16 [128, 256, 64], P('groups', 'row'), parts along dimension 0, may hold values from -6 to 6
- pair_state_tiles: bfloat16 [512, 256, 128], P(('groups', 'row')), parts along dimension 0, may hold values from -6 to 6
- alignment_mask: int32 [128, 256], P('groups', 'row'), parts along dimension 0, may hold values 0 or 1
- token_real_mask: int32 [512], P('groups'), parts along dimension 0, may hold values 0 or 1
- lineup_standardize_scaling: float32 [64], replicated, may hold values from 0.1 to 1.9
- former_factor_proj: bfloat16 [64, 32], replicated, may hold values from -0.75 to 0.75
- latter_factor_proj: bfloat16 [64, 32], replicated, may hold values from -0.75 to 0.75
- outer_output_weight: bfloat16 [1024, 128], replicated, may hold values from -0.1875 to 0.1875
- pair_norm_gain: float32 [128], replicated, may hold values from 0.1 to 1.9
- pair_logit_weight: float32 [128, 8], replicated
- content_vector_proj: bfloat16 [64, 256], replicated, may hold values from -0.75 to 0.75
- sigmoid_switch_proj: bfloat16 [64, 256], replicated, may hold values from -0.75 to 0.75
- final_result_proj: bfloat16 [256, 64], replicated, may hold values from -0.375 to 0.375
Outputs:
- alignment_updated: bfloat16 [128, 256, 64], P('groups', 'row'), parts along dimension 0
- pair_updated: bfloat16 [512, 256, 128], P(('groups', 'row')), parts along dimension 0
The draws below stay inside these ranges and needn't reach their ends.
There are 2 independent parts, one for each index of `groups`. The reference program is written for one: setup_inputs(seed, part) draws one part's arguments, and reference() takes and returns one part's arrays. A program takes and returns all parts, laid end to end along the dimension named above; an argument that names none is the same for every part. Nothing has to cross between parts.
All inputs are finite; a program needn't handle non-finite values. No bound on the sum of `alignment_mask` on one device may be relied on, other than what follows from the above.
Results may differ from the reference program's by a relative error of at most 0.007.
Values may be sent and summed in bfloat16 or wider, within the bound.
No kernel may reach another device: no remote copies, remote signals or barrier semaphores. Data moves between devices by JAX's collectives and lax.ppermute only.
A program may use at most 128 MiB of HBM per device.

```python
import math
import jax
import jax.numpy as jnp
from jax import lax

LINEUP_FEATURES = 64
C_Z = 128
PRODUCT_FEATURES = 32
AVERAGER_GROUPS = 8
GROUP_FEATURES = 32
HOMOLOG_TOTAL = 64
CROP_RESIDUE_NUM = 256


def draw_pair_logit_weight(key, part):
    first, second = jax.random.split(jax.random.fold_in(key, 7))
    scales = jnp.exp(jax.random.uniform(first, (AVERAGER_GROUPS,), jnp.float32, math.log(0.5), math.log(8.0)))
    entries = jax.random.normal(second, (C_Z, AVERAGER_GROUPS), jnp.float32)
    return entries * scales[None, :] / math.sqrt(C_Z)


def set_ends(values, stream_key, low, high):
    dims = values.shape
    spot = [jax.random.randint(jax.random.fold_in(stream_key, axis), (), 0, dims[axis]) for axis in range(len(dims))]
    values = values.at[tuple(spot)].set(low)
    longest = dims.index(max(dims))
    spot[longest] = (spot[longest] + 1) % dims[longest]
    return values.at[tuple(spot)].set(high)


def block_scale(stream_key, shape, shards, least, high):
    loudness = 1.0
    for axis_at, blocks in shards:
        heights = jax.random.uniform(jax.random.fold_in(jax.random.fold_in(stream_key, 6), axis_at), (blocks,), jnp.float32, least / len(shards), high / len(shards))
        loudness = loudness * jnp.repeat(jnp.exp(heights), shape[axis_at] // blocks).reshape((-1,) + (1,) * (len(shape) - 1 - axis_at))
    return loudness


def noise(stream_key, extent, scale, limit, cuts=(), dtype=jnp.bfloat16):
    loudness = block_scale(stream_key, extent, cuts, -0.22, 0.18) if cuts else 1.0
    result = jax.random.normal(stream_key, extent, jnp.float32) * scale * loudness
    return jnp.minimum(jnp.maximum(result, -limit), limit).astype(dtype)


def setup_inputs(seed: int = 0, part: int = 0) -> dict:
    key_list = jax.random.split(jax.random.key(seed), 14)
    part_splits = jax.random.split(jax.random.fold_in(key_list[13], part), 14)
    return {
        "homolog_embedding": noise(part_splits[0], (HOMOLOG_TOTAL, CROP_RESIDUE_NUM, LINEUP_FEATURES), 1.0, 6.0, ((1, 16),)),
        "pair_state_tiles": noise(part_splits[1], (CROP_RESIDUE_NUM, CROP_RESIDUE_NUM, C_Z), 1.0, 6.0, ((0, 16),)),
        "alignment_mask": set_ends((jax.random.randint(part_splits[2], (HOMOLOG_TOTAL, CROP_RESIDUE_NUM), 0, 4) < 3).astype(jnp.int32), jax.random.fold_in(part_splits[2], 1), 0, 1),
        "token_real_mask": set_ends((jax.random.randint(part_splits[3], (CROP_RESIDUE_NUM,), 0, 8) < 7).astype(jnp.int32), jax.random.fold_in(part_splits[3], 1), 0, 1),
        "lineup_standardize_scaling": jnp.clip(1.0 + 0.18 * jax.random.normal(key_list[4], (LINEUP_FEATURES,), jnp.float32), 0.1, 1.9),
        "former_factor_proj": noise(key_list[5], (LINEUP_FEATURES, PRODUCT_FEATURES), LINEUP_FEATURES ** -0.5, 0.75),
        "latter_factor_proj": noise(key_list[6], (LINEUP_FEATURES, PRODUCT_FEATURES), LINEUP_FEATURES ** -0.5, 0.75),
        "outer_output_weight": noise(key_list[7], (PRODUCT_FEATURES * PRODUCT_FEATURES, C_Z), (PRODUCT_FEATURES * PRODUCT_FEATURES) ** -0.5, 0.1875),
        "pair_norm_gain": jnp.clip(1.0 + 0.18 * jax.random.normal(key_list[8], (C_Z,), jnp.float32), 0.1, 1.9),
        "pair_logit_weight": draw_pair_logit_weight(jax.random.fold_in(key_list[13], 71), part),
        "content_vector_proj": noise(key_list[10], (LINEUP_FEATURES, AVERAGER_GROUPS * GROUP_FEATURES), LINEUP_FEATURES ** -0.5, 0.75),
        "sigmoid_switch_proj": noise(key_list[11], (LINEUP_FEATURES, AVERAGER_GROUPS * GROUP_FEATURES), LINEUP_FEATURES ** -0.5, 0.75),
        "final_result_proj": noise(key_list[12], (AVERAGER_GROUPS * GROUP_FEATURES, LINEUP_FEATURES), (AVERAGER_GROUPS * GROUP_FEATURES) ** -0.5, 0.375),
    }


def layer_normalize(inputs, gain):
    inputs = inputs.astype(jnp.float32)
    center = lax.optimization_barrier(jnp.mean(inputs, axis=-1, keepdims=True))
    spread = lax.optimization_barrier(jnp.mean((inputs - center) ** 2, axis=-1, keepdims=True))
    return (inputs - center) * lax.rsqrt(spread + 1e-05) * gain

def reference(homolog_embedding, pair_state_tiles, alignment_mask, token_real_mask, lineup_standardize_scaling, former_factor_proj, latter_factor_proj, outer_output_weight, pair_norm_gain, pair_logit_weight, content_vector_proj, sigmoid_switch_proj, final_result_proj):
    single_float = jnp.float32
    normed_input = layer_normalize(homolog_embedding, lineup_standardize_scaling).astype(jnp.bfloat16)
    normed_f = normed_input.astype(single_float)
    mask_floating = alignment_mask.astype(single_float)
    left_rows = (jnp.einsum('snc,cd->snd', normed_f, former_factor_proj.astype(single_float)) * mask_floating[:, :, None]).astype(jnp.bfloat16)
    right_rows = (jnp.einsum('snc,cd->snd', normed_f, latter_factor_proj.astype(single_float)) * mask_floating[:, :, None]).astype(jnp.bfloat16)
    tokens = CROP_RESIDUE_NUM
    width = math.gcd(tokens, 64)
    nblocks = tokens // width
    weight_cube = outer_output_weight.astype(single_float).reshape(PRODUCT_FEATURES, PRODUCT_FEATURES, C_Z)
    left_blocks = left_rows.reshape(HOMOLOG_TOTAL, nblocks, width, PRODUCT_FEATURES).transpose(1, 0, 2, 3)
    mask_blocks = mask_floating.reshape(HOMOLOG_TOTAL, nblocks, width).transpose(1, 0, 2)
    right_f = right_rows.astype(single_float)

    def one_block(operands):
        block_left, block_mask = operands
        folded = jnp.einsum('sic,cez->seiz', block_left.astype(single_float), weight_cube).astype(jnp.bfloat16)
        product = jnp.einsum('seiz,sje->ijz', folded.astype(single_float), right_f)
        counts = jnp.einsum('si,sj->ij', block_mask, mask_floating)
        return product / (1.0 + counts)[:, :, None]
    update = lax.map(one_block, (left_blocks, mask_blocks)).reshape(tokens, tokens, C_Z)
    pair_updated = (pair_state_tiles.astype(single_float) + update).astype(jnp.bfloat16)
    pair_normed = layer_normalize(pair_updated, pair_norm_gain)
    logits = jnp.einsum('ijc,ch->hij', pair_normed, pair_logit_weight, precision=lax.Precision.HIGHEST)
    logits = jnp.where(token_real_mask[None, None, :] == 1, logits, -1000000000.0)
    weights = jax.nn.softmax(logits, axis=2).astype(jnp.bfloat16)
    values = jnp.einsum('snc,ck->snk', normed_f, content_vector_proj.astype(single_float)).astype(jnp.bfloat16)
    gate_vals = jax.nn.sigmoid(jnp.einsum('snc,ck->snk', normed_f, sigmoid_switch_proj.astype(single_float)))
    values_heads = values.astype(single_float).reshape(HOMOLOG_TOTAL, tokens, AVERAGER_GROUPS, GROUP_FEATURES)
    average = jnp.einsum('hij,sjhc->sihc', weights.astype(single_float), values_heads).reshape(HOMOLOG_TOTAL, tokens, AVERAGER_GROUPS * GROUP_FEATURES)
    gated_output = (gate_vals * average).astype(jnp.bfloat16)
    update_alignment = jnp.einsum('tpb,bo->tpo', gated_output.astype(single_float), final_result_proj.astype(single_float))
    alignment_updated = (homolog_embedding.astype(single_float) + update_alignment).astype(jnp.bfloat16)
    return (alignment_updated, pair_updated)
```

```python
import functools

import jax
import jax.numpy as jnp
from jax import lax
from jax.experimental import pallas as pl
from jax.experimental.pallas import tpu as pltpu
from jax.sharding import PartitionSpec as P

F32 = jnp.float32
BF16 = jnp.bfloat16
VM = pl.BlockSpec(memory_space=pltpu.VMEM)
HB = pl.BlockSpec(memory_space=pl.ANY)


def dot(a, b):
    return jnp.dot(a, b, preferred_element_type=F32)


def dot_nt(a, b):
    return lax.dot_general(a, b, (((1,), (1,)), ((), ())), preferred_element_type=F32)


def iota(shape, axis):
    return lax.broadcasted_iota(jnp.int32, shape, axis)


def split(x):
    high = x.astype(BF16)
    return high, (x - high.astype(F32)).astype(BF16)


def twice(block):
    zero = jnp.zeros_like(block)
    return jnp.concatenate(
        [jnp.concatenate([block, zero], 1), jnp.concatenate([zero, block], 1)], 0
    )


def pack_kernel(rows_ref, mask_ref, gain_ref, out_ref):
    seqs, toks, width = rows_ref.shape
    outer = seqs // 8
    x = rows_ref[...].reshape(outer, 2, 4, toks, width)
    x = jnp.concatenate([x[:, 0], x[:, 1]], axis=-1).reshape(seqs // 2 * toks, 2 * width)
    lanes = 2 * width
    same = (iota((lanes, lanes), 0) // width) == (iota((lanes, lanes), 1) // width)
    mean_of = jnp.where(same, 1.0 / width, 0.0).astype(BF16)
    centered = x.astype(F32) - dot(x, mean_of)
    high, low = split(centered * centered)
    spread = dot(high, mean_of) + dot(low, mean_of)
    gain = jnp.concatenate([gain_ref[...], gain_ref[...]], axis=-1)
    normed = centered * lax.rsqrt(spread + 1e-05) * gain
    out_ref[: seqs // 2] = normed.astype(BF16).reshape(seqs // 2, toks, lanes)
    mask = mask_ref[...].astype(F32)
    if seqs < lanes:
        mask = jnp.concatenate([mask, jnp.zeros((toks, lanes - seqs), F32)], axis=-1)
    out_ref[seqs // 2] = mask.astype(BF16)


def fold_kernel(
    seqs,
    heads,
    pack_ref,
    former_ref,
    latter_ref,
    outer_ref,
    content_ref,
    switch_ref,
    final_ref,
    folded_ref,
    gate_ref,
    right_ref,
    value_ref,
    result_ref,
    weight_scr,
    left_scr,
    lhs_scr,
):
    half, toks, lanes = seqs // 2, pack_ref.shape[1], pack_ref.shape[2]
    width, factor = former_ref.shape
    outer = seqs // 8
    rows = pack_ref[:half].reshape(half * toks, lanes)
    left = dot(rows, twice(former_ref[...]))
    for so in range(outer):
        for s2 in range(2):
            left_scr[pl.ds((so * 8 + s2 * 4) * toks, 4 * toks), :factor] = left[
                so * 4 * toks : (so + 1) * 4 * toks, s2 * factor : (s2 + 1) * factor
            ]
    eye = iota((seqs, seqs), 0) == iota((seqs, seqs), 1)
    mask = pack_ref[half].astype(F32)[:, :seqs]
    for i in range(toks):
        picked = jnp.where(eye, jnp.broadcast_to(mask[i : i + 1], (seqs, seqs)), 0.0)
        rows_i = left_scr[pl.ds(i, seqs, stride=toks), :][:, :factor].astype(BF16)
        lhs_scr[i * seqs : (i + 1) * seqs, :] = dot(picked.astype(BF16), rows_i).astype(BF16)
    weight_scr[...] = outer_ref[...].astype(F32)
    channels = outer_ref.shape[1]

    def step(m, carry):
        even = weight_scr[pl.ds(2 * m, factor, stride=factor), :]
        odd = weight_scr[pl.ds(2 * m + 1, factor, stride=factor), :]
        pair = jnp.concatenate([even, odd], axis=1).astype(BF16)
        for i in range(toks):
            block = dot(lhs_scr[i * seqs : (i + 1) * seqs, :], pair)
            block = block.reshape(outer, 8, 2 * channels)
            block = jnp.concatenate([block[:, :, :channels], block[:, :, channels:]], axis=1)
            folded_ref[i, :, pl.ds(pl.multiple_of(16 * m, 16), 16), :] = block.astype(BF16)
        return carry

    lax.fori_loop(0, factor // 2, step, 0)

    spread = jnp.where(
        iota((factor, 8 * factor), 0) == iota((factor, 8 * factor), 1) // 8, 1.0, 0.0
    ).astype(BF16)
    wide = dot(latter_ref[...], spread)
    lane = iota(wide.shape, 1) % 8
    for rest in range(4):
        for s2 in range(2):
            base = (rest * 2 + s2) * width
            right_ref[base : base + width, :] = jnp.where(lane == s2 * 4 + rest, wide, 0.0).astype(
                BF16
            )
    column = content_ref.shape[1] // heads
    for hp in range(heads // 2):
        cols = slice(2 * column * hp, 2 * column * (hp + 1))
        gate_ref[hp] = jax.nn.sigmoid(dot(rows, twice(switch_ref[:, cols])))
        piece = content_ref[:, cols].astype(F32)
        which = iota(piece.shape, 1) // column
        zero = jnp.zeros_like(piece)
        for h2 in range(2):
            mine = jnp.where(which == h2, piece, 0.0)
            for s2 in range(2):
                base = (h2 * 2 + s2) * width
                row = [mine, zero] if s2 == 0 else [zero, mine]
                value_ref[hp, base : base + width, :] = jnp.concatenate(row, 1).astype(BF16)
        result_ref[hp] = twice(final_ref[cols, :])


def main_kernel(
    seqs,
    heads,
    shifts,
    *refs,
):
    blocks = refs[: len(shifts)]
    (
        rows_ref,
        state_ref,
        real_ref,
        logit_ref,
        folded_ref,
        gate_ref,
        right_ref,
        value_ref,
        result_ref,
        out_ref,
        pair_ref,
        all_scr,
        state_scr,
        rhs_scr,
        inverse_scr,
        logits_scr,
        mixed_scr,
        sems,
        state_sem,
        pair_sem,
    ) = refs[len(shifts) :]
    half = seqs // 2
    outer = seqs // 8
    _, devs, toks, lanes = all_scr.shape
    tokens = devs * toks
    me = lax.axis_index("row")

    def place(shift):
        where = 0
        bit = 1
        while bit < devs:
            mine = (me // bit) % 2
            where = where + bit * ((1 - mine) if shift & bit else mine)
            bit *= 2
        return where

    spots = [place(k) for k in shifts]
    order = [(half, 1)] + [(so * 4, 4) for so in range(outer)]
    for n, (first, count) in enumerate(order):
        for spot, block in zip(spots, blocks):
            pltpu.make_async_copy(
                block.at[pl.ds(first, count)],
                all_scr.at[pl.ds(first, count), spot],
                sems.at[n],
            ).start()
    load_state = pltpu.make_async_copy(state_ref, state_scr, state_sem)
    load_state.start()

    def arrived(n):
        first, count = order[n]
        slab = all_scr.at[pl.ds(first, count)]
        pltpu.make_async_copy(slab, slab, sems.at[n]).wait()

    arrived(0)
    mask = all_scr[half].reshape(tokens, lanes)
    own = all_scr[half, pl.ds(me, 1)].reshape(toks, lanes)
    inverse_scr[...] = 1.0 / (1.0 + dot_nt(mask, own))
    wide = right_ref.shape[1]
    which = iota((lanes, wide), 0) - iota((lanes, wide), 1) % 8
    for so in range(outer):
        pick = jnp.where(which == 8 * so, 1.0, 0.0).astype(BF16)
        mask_wide = dot(mask, pick)
        arrived(1 + so)
        rows = jnp.concatenate(
            [all_scr[so * 4 + r].reshape(tokens, lanes) for r in range(4)], axis=1
        )
        rhs_scr[:, so * wide : (so + 1) * wide] = (dot(rows, right_ref[...]) * mask_wide).astype(
            BF16
        )
    load_state.wait()
    weights = logit_ref[...]
    w_high, w_low = split(weights)
    lhs = jnp.concatenate(
        [
            jnp.concatenate([w_high, w_high], axis=1),
            jnp.concatenate([w_low, jnp.zeros_like(w_low)], axis=1),
        ],
        axis=0,
    )
    channels = folded_ref.shape[-1]
    for i in range(toks):
        acc = dot(rhs_scr[...], folded_ref[i].reshape(outer * wide, channels))
        x = state_scr[i].astype(F32) + acc * inverse_scr[:, i : i + 1]
        x = x.astype(BF16)
        state_scr[i] = x
        pltpu.make_async_copy(state_scr.at[i], pair_ref.at[i], pair_sem.at[i]).start()
        x = x.astype(F32)
        x = x - jnp.mean(x, axis=-1, keepdims=True)
        spread = jnp.mean(x * x, axis=-1, keepdims=True)
        high, low = split(x * lax.rsqrt(spread + 1e-05))
        logits = dot_nt(lhs, jnp.concatenate([high, low], axis=1))
        logits = logits[:heads] + logits[heads:]
        for jb in range(tokens // 128):
            logits_scr[jb, pl.ds(i, heads, stride=toks), :] = logits[:, jb * 128 : jb * 128 + 128]
    logits = jnp.concatenate([logits_scr[jb] for jb in range(tokens // 128)], axis=1)
    logits = jnp.where(real_ref[...] == 1, logits, -1000000000.0)
    top = jnp.max(logits, axis=-1, keepdims=True)
    power = jnp.exp(logits - top)
    probs = (power / jnp.sum(power, axis=-1, keepdims=True)).astype(BF16)
    for b in range(0, half, 2):
        values = jnp.concatenate(
            [all_scr[b].reshape(tokens, lanes), all_scr[b + 1].reshape(tokens, lanes)], axis=1
        )
        mixed = dot(probs, values).astype(BF16)
        mixed_scr[b] = mixed[:, :lanes]
        mixed_scr[b + 1] = mixed[:, lanes:]
    total = None
    for hp in range(heads // 2):
        pair = jnp.concatenate(
            [
                mixed_scr[:, (2 * hp + h2) * toks : (2 * hp + h2 + 1) * toks, :].reshape(
                    half * toks, lanes
                )
                for h2 in range(2)
            ],
            axis=1,
        )
        average = dot(pair, value_ref[hp])
        gated = (gate_ref[hp] * average).astype(BF16)
        part = dot(gated, result_ref[hp])
        total = part if total is None else total + part
    width = rows_ref.shape[2]
    total = total.reshape(outer, 4, toks, lanes)
    base = rows_ref[...].astype(F32).reshape(outer, 2, 4, toks, width)
    for s2 in range(2):
        piece = base[:, s2] + total[..., s2 * width : (s2 + 1) * width]
        for so in range(outer):
            out_ref[so * 8 + s2 * 4 : so * 8 + s2 * 4 + 4] = piece[so].astype(BF16)
    for i in range(toks):
        pltpu.make_async_copy(state_scr.at[i], pair_ref.at[i], pair_sem.at[i]).wait()


def shards(
    homolog_embedding,
    pair_state_tiles,
    alignment_mask,
    token_real_mask,
    lineup_standardize_scaling,
    former_factor_proj,
    latter_factor_proj,
    outer_output_weight,
    pair_norm_gain,
    pair_logit_weight,
    content_vector_proj,
    sigmoid_switch_proj,
    final_result_proj,
    *,
    devs,
):
    seqs, toks, width = homolog_embedding.shape
    tokens = devs * toks
    heads = pair_logit_weight.shape[1]
    factor = former_factor_proj.shape[1]
    channels = outer_output_weight.shape[1]
    lanes = 2 * width
    half, outer = seqs // 2, seqs // 8
    params = pltpu.CompilerParams(vmem_limit_bytes=28 << 20)
    packed = pl.pallas_call(
        pack_kernel,
        out_shape=jax.ShapeDtypeStruct((half + 1, toks, lanes), BF16),
        in_specs=[VM] * 3,
        out_specs=VM,
        compiler_params=params,
        name="pack",
    )(homolog_embedding, alignment_mask.T, lineup_standardize_scaling[None])

    def swap(block, shift):
        return lax.ppermute(block, "row", [(n, n ^ shift) for n in range(devs)])

    held = {0: packed}
    for shift in sorted(range(4, devs, 4), reverse=True):
        held[shift] = swap(packed, shift)
    for bit in (2, 1):
        for shift in sorted(held):
            held[shift ^ bit] = swap(held[shift], bit)
    shifts = tuple(sorted(held))

    folded, gate, right, value, result = pl.pallas_call(
        functools.partial(fold_kernel, seqs, heads),
        out_shape=(
            jax.ShapeDtypeStruct((toks, outer, 8 * factor, channels), BF16),
            jax.ShapeDtypeStruct((heads // 2, half * toks, lanes), F32),
            jax.ShapeDtypeStruct((8 * width, 8 * factor), BF16),
            jax.ShapeDtypeStruct((heads // 2, 4 * width, lanes), BF16),
            jax.ShapeDtypeStruct((heads // 2, lanes, lanes), BF16),
        ),
        in_specs=[VM] * 7,
        out_specs=(VM,) * 5,
        scratch_shapes=[
            pltpu.VMEM(outer_output_weight.shape, F32),
            pltpu.VMEM((seqs * toks, 128), F32),
            pltpu.VMEM((seqs * toks, factor), BF16),
        ],
        compiler_params=params,
        cost_estimate=pl.CostEstimate(
            flops=10**9, bytes_accessed=10**7, transcendentals=10**6
        ),
        name="fold",
    )(
        packed,
        former_factor_proj,
        latter_factor_proj,
        outer_output_weight,
        content_vector_proj,
        sigmoid_switch_proj,
        final_result_proj,
    )
    scaled = (pair_norm_gain[:, None] * pair_logit_weight).T
    out, pair = pl.pallas_call(
        functools.partial(main_kernel, seqs, heads, shifts),
        out_shape=(
            jax.ShapeDtypeStruct(homolog_embedding.shape, BF16),
            jax.ShapeDtypeStruct(pair_state_tiles.shape, BF16),
        ),
        in_specs=[HB] * devs + [VM, HB] + [VM] * 7,
        out_specs=(VM, HB),
        scratch_shapes=[
            pltpu.VMEM((half + 1, devs, toks, lanes), BF16),
            pltpu.VMEM(pair_state_tiles.shape, BF16),
            pltpu.VMEM((tokens, outer * 8 * factor), BF16),
            pltpu.VMEM((tokens, toks), F32),
            pltpu.VMEM((tokens // 128, heads * toks, 128), F32),
            pltpu.VMEM((half, heads * toks, lanes), BF16),
            pltpu.SemaphoreType.DMA((outer + 1,)),
            pltpu.SemaphoreType.DMA,
            pltpu.SemaphoreType.DMA((toks,)),
        ],
        compiler_params=params,
        cost_estimate=pl.CostEstimate(
            flops=4 * 10**9, bytes_accessed=10**7, transcendentals=10**6
        ),
        name="main",
    )(
        *[held[shift] for shift in shifts],
        homolog_embedding,
        pair_state_tiles,
        token_real_mask[None],
        scaled,
        folded,
        gate,
        right,
        value,
        result,
    )
    return out, pair


def solution(mesh):
    placed = (
        P("groups", "row", None),
        P(("groups", "row"), None, None),
        P("groups", "row"),
        P("groups"),
        P(),
        P(),
        P(),
        P(),
        P(),
        P(),
        P(),
        P(),
        P(),
    )
    return jax.shard_map(
        functools.partial(shards, devs=mesh.shape["row"]),
        mesh=mesh,
        in_specs=placed,
        out_specs=(P("groups", "row", None), P(("groups", "row"), None, None)),
        check_vma=False,
    )
```

```python
import functools

import jax
import jax.numpy as jnp
from jax import lax
from jax.experimental import pallas as pl
from jax.experimental.pallas import tpu as pltpu
from jax.sharding import PartitionSpec as P


F32 = jnp.float32
BF16 = jnp.bfloat16
VM = pl.BlockSpec(memory_space=pltpu.VMEM)
HB = pl.BlockSpec(memory_space=pltpu.HBM)


def dot(a, b):
    return jnp.dot(a, b, preferred_element_type=F32)


def dot_nt(a, b):
    return lax.dot_general(a, b, (((1,), (1,)), ((), ())), preferred_element_type=F32)


def iota(shape, axis):
    return lax.broadcasted_iota(jnp.int32, shape, axis)


def split(x):
    high = x.astype(BF16)
    return high, (x - high.astype(F32)).astype(BF16)


def twice(block):
    zero = jnp.zeros_like(block)
    return jnp.concatenate(
        [jnp.concatenate([block, zero], 1), jnp.concatenate([zero, block], 1)], 0
    )


def fetch(sources, targets, sems):
    copies = [pltpu.make_async_copy(a, b, sems.at[n]) for n, (a, b) in enumerate(zip(sources, targets))]
    for copy in copies:
        copy.start()
    return copies


def pack_kernel(rows_hbm, mask_hbm, gain_hbm, real_hbm, out_ref, rows_ref, mask_ref, gain_ref, real_ref, sems):
    copies = fetch(
        (rows_hbm, mask_hbm, gain_hbm, real_hbm), (rows_ref, mask_ref, gain_ref, real_ref), sems
    )
    for copy in copies:
        copy.wait()
    seqs, toks, width = rows_ref.shape
    outer = seqs // 8
    x = rows_ref[...].reshape(outer, 2, 4, toks, width)
    x = jnp.concatenate([x[:, 0], x[:, 1]], axis=-1).reshape(seqs // 2 * toks, 2 * width)
    lanes = 2 * width
    same = (iota((lanes, lanes), 0) // width) == (iota((lanes, lanes), 1) // width)
    mean_of = jnp.where(same, 1.0 / width, 0.0).astype(BF16)
    centered = x.astype(F32) - dot(x, mean_of)
    high, low = split(centered * centered)
    spread = dot(high, mean_of) + dot(low, mean_of)
    gain = jnp.concatenate([gain_ref[...], gain_ref[...]], axis=-1)
    normed = centered * lax.rsqrt(spread + 1e-05) * gain
    out_ref[: seqs // 2] = normed.astype(BF16).reshape(seqs // 2, toks, lanes)
    real = real_ref[...].astype(F32)
    tokens = real.shape[1]
    here = iota((toks, tokens), 1) == lax.axis_index("row") * toks + iota((toks, tokens), 0)
    mine = jnp.sum(jnp.where(here, real, 0.0), axis=1, keepdims=True)
    mask = mask_ref[...].astype(F32)
    mask = jnp.concatenate([mask, jnp.zeros((toks, lanes - seqs), F32)], axis=-1)
    mask = jnp.where(iota(mask.shape, 1) == seqs, mine, mask)
    out_ref[seqs // 2] = mask.astype(BF16)


def fold_kernel(
    seqs,
    heads,
    pack_ref,
    former_hbm,
    latter_hbm,
    outer_hbm,
    content_hbm,
    switch_hbm,
    final_hbm,
    folded_ref,
    gate_ref,
    right_ref,
    value_ref,
    result_ref,
    former_ref,
    latter_ref,
    outer_ref,
    content_ref,
    switch_ref,
    final_ref,
    weight_scr,
    left_scr,
    lhs_scr,
    sems,
):
    copies = fetch(
        (former_hbm, outer_hbm, latter_hbm, content_hbm, switch_hbm, final_hbm),
        (former_ref, outer_ref, latter_ref, content_ref, switch_ref, final_ref),
        sems,
    )
    half, toks, lanes = seqs // 2, pack_ref.shape[1], pack_ref.shape[2]
    factor, width = former_ref.shape
    outer = seqs // 8
    rows = pack_ref[:half].reshape(half * toks, lanes)
    copies[0].wait()
    left = dot_nt(rows, twice(former_ref[...]))
    for so in range(outer):
        for s2 in range(2):
            left_scr[pl.ds((so * 8 + s2 * 4) * toks, 4 * toks), :factor] = left[
                so * 4 * toks : (so + 1) * 4 * toks, s2 * factor : (s2 + 1) * factor
            ]
    eye = iota((seqs, seqs), 0) == iota((seqs, seqs), 1)
    mask = pack_ref[half].astype(F32)[:, :seqs]
    for i in range(toks):
        picked = jnp.where(eye, jnp.broadcast_to(mask[i : i + 1], (seqs, seqs)), 0.0)
        rows_i = left_scr[pl.ds(i, seqs, stride=toks), :][:, :factor].astype(BF16)
        lhs_scr[i * seqs : (i + 1) * seqs, :] = dot(picked.astype(BF16), rows_i).astype(BF16)
    copies[1].wait()
    weight_scr[...] = outer_ref[...].astype(F32)
    channels = outer_ref.shape[1]

    def step(m, carry):
        even = weight_scr[pl.ds(2 * m, factor, stride=factor), :]
        odd = weight_scr[pl.ds(2 * m + 1, factor, stride=factor), :]
        pair = jnp.concatenate([even, odd], axis=1).astype(BF16)
        for i in range(toks):
            block = dot(lhs_scr[i * seqs : (i + 1) * seqs, :], pair)
            block = block.reshape(outer, 8, 2 * channels)
            block = jnp.concatenate([block[:, :, :channels], block[:, :, channels:]], axis=1)
            first = i % 2 * channels
            folded_ref[
                i // 2, :, pl.ds(pl.multiple_of(16 * m, 16), 16), first : first + channels
            ] = block.astype(BF16)
        return carry

    lax.fori_loop(0, factor // 2, step, 0)
    for copy in copies[2:]:
        copy.wait()
    spread = jnp.where(
        iota((factor, 8 * factor), 0) == iota((factor, 8 * factor), 1) // 8, 1.0, 0.0
    ).astype(BF16)
    wide = dot(latter_ref[...].astype(F32).T.astype(BF16), spread)
    lane = iota(wide.shape, 1) % 8
    for rest in range(4):
        for s2 in range(2):
            base = (rest * 2 + s2) * width
            right_ref[base : base + width, :] = jnp.where(lane == s2 * 4 + rest, wide, 0.0).astype(
                BF16
            )
    column = content_ref.shape[1] // heads
    for hp in range(heads // 2):
        cols = slice(2 * column * hp, 2 * column * (hp + 1))
        gate_ref[hp] = jax.nn.sigmoid(dot(rows, twice(switch_ref[:, cols])))
        piece = content_ref[:, cols].astype(F32)
        which = iota(piece.shape, 1) // column
        zero = jnp.zeros_like(piece)
        for h2 in range(2):
            mine = jnp.where(which == h2, piece, 0.0)
            for s2 in range(2):
                base = (h2 * 2 + s2) * width
                row = [mine, zero] if s2 == 0 else [zero, mine]
                value_ref[hp, base : base + width, :] = jnp.concatenate(row, 1).astype(BF16)
        result_ref[hp] = twice(final_ref[:, cols])


def main_kernel(seqs, heads, shifts, *refs):
    blocks = refs[: len(shifts)]
    (
        rows_hbm,
        state_hbm,
        weight_hbm,
        gain_hbm,
        folded_ref,
        gate_ref,
        right_ref,
        value_ref,
        result_ref,
        out_ref,
        pair_hbm,
        rows_ref,
        state_ref,
        weight_ref,
        gain_ref,
        pair_ref,
        wide_scr,
        rhs_scr,
        logits_scr,
        mixed_scr,
        sems,
        pair_sem,
    ) = refs[len(shifts) :]
    copies = fetch(
        (weight_hbm, gain_hbm, state_hbm, rows_hbm),
        (weight_ref, gain_ref, state_ref, rows_ref),
        sems,
    )
    half = seqs // 2
    outer = seqs // 8
    devs = len(shifts)
    _, toks, lanes = blocks[0].shape
    tokens = devs * toks
    me = lax.axis_index("row")

    def place(shift):
        where = 0
        bit = 1
        while bit < devs:
            mine = (me // bit) % 2
            where = where + bit * ((1 - mine) if shift & bit else mine)
            bit *= 2
        return pl.multiple_of(where * toks, toks)

    spots = [place(k) for k in shifts]

    def gathered(n):
        return jnp.concatenate([block[n] for block in blocks], axis=0)

    mask = gathered(half)
    inverse = 1.0 / (1.0 + dot_nt(mask, jnp.where(iota((toks, lanes), 1) < seqs, blocks[0][half], 0)))
    real = dot_nt(jnp.where(iota((8, lanes), 1) == seqs, 1.0, 0.0).astype(BF16), mask)
    wide = right_ref.shape[1]
    which = iota((lanes, wide), 0) - iota((lanes, wide), 1) % 8
    for so in range(outer):
        pick = jnp.where(which == 8 * so, 1.0, 0.0).astype(BF16)
        wide_scr[:, so * wide : (so + 1) * wide] = dot(mask, pick).astype(BF16)
    for so in range(outer):
        rows = jnp.concatenate([gathered(so * 4 + r) for r in range(4)], axis=1)
        cols = slice(so * wide, (so + 1) * wide)
        rhs_scr[:, cols] = (dot(rows, right_ref[...]) * wide_scr[:, cols].astype(F32)).astype(BF16)
    for copy in copies:
        copy.wait()
    w_high, w_low = split(weight_ref[...] * gain_ref[...])
    lhs = jnp.concatenate(
        [
            jnp.concatenate([w_high, w_high], axis=1),
            jnp.concatenate([w_low, jnp.zeros_like(w_low)], axis=1),
        ],
        axis=0,
    )
    channels = state_ref.shape[-1]

    def product(ip):
        return dot(rhs_scr[...], folded_ref[ip].reshape(outer * wide, 2 * channels))

    acc = product(0)
    for ip in range(toks // 2):
        later = product(ip + 1) if ip + 1 < toks // 2 else None
        for i2 in range(2):
            i = 2 * ip + i2
            x = jnp.concatenate([state_ref[i, pl.ds(spot, toks), :] for spot in spots], axis=0)
            x = x.astype(F32) + acc[:, i2 * channels : (i2 + 1) * channels] * inverse[:, i : i + 1]
            x = x.astype(BF16)
            for n, spot in enumerate(spots):
                pair_ref[i, pl.ds(spot, toks), :] = x[n * toks : (n + 1) * toks]
            pltpu.make_async_copy(pair_ref.at[i], pair_hbm.at[i], pair_sem.at[i]).start()
            x = x.astype(F32)
            x = x - jnp.mean(x, axis=-1, keepdims=True)
            spread = jnp.mean(x * x, axis=-1, keepdims=True)
            high, low = split(x * lax.rsqrt(spread + 1e-05))
            logits = dot_nt(lhs, jnp.concatenate([high, low], axis=1))
            logits = logits[:heads] + logits[heads:]
            for jb in range(tokens // 128):
                logits_scr[jb, pl.ds(i, heads, stride=toks), :] = logits[
                    :, jb * 128 : jb * 128 + 128
                ]
        acc = later
    logits = jnp.concatenate([logits_scr[jb] for jb in range(tokens // 128)], axis=1)
    logits = jnp.where(real[:1] > 0.5, logits, -1000000000.0)
    top = jnp.max(logits, axis=-1, keepdims=True)
    power = jnp.exp(logits - top)
    probs = (power / jnp.sum(power, axis=-1, keepdims=True)).astype(BF16)
    for b in range(0, half, 2):
        mixed = dot(probs, jnp.concatenate([gathered(b), gathered(b + 1)], axis=1)).astype(BF16)
        mixed_scr[b] = mixed[:, :lanes]
        mixed_scr[b + 1] = mixed[:, lanes:]
    total = None
    for hp in range(heads // 2):
        pair = jnp.concatenate(
            [
                mixed_scr[:, (2 * hp + h2) * toks : (2 * hp + h2 + 1) * toks, :].reshape(
                    half * toks, lanes
                )
                for h2 in range(2)
            ],
            axis=1,
        )
        average = dot(pair, value_ref[hp])
        gated = (gate_ref[hp] * average).astype(BF16)
        part = dot_nt(gated, result_ref[hp])
        total = part if total is None else total + part
    width = rows_ref.shape[2]
    total = total.reshape(outer, 4, toks, lanes)
    base = rows_ref[...].astype(F32).reshape(outer, 2, 4, toks, width)
    for s2 in range(2):
        piece = base[:, s2] + total[..., s2 * width : (s2 + 1) * width]
        for so in range(outer):
            out_ref[so * 8 + s2 * 4 : so * 8 + s2 * 4 + 4] = piece[so].astype(BF16)
    for i in range(toks):
        pltpu.make_async_copy(pair_ref.at[i], pair_hbm.at[i], pair_sem.at[i]).wait()


def shards(
    homolog_embedding,
    pair_state_tiles,
    alignment_mask,
    token_real_mask,
    lineup_standardize_scaling,
    former_factor_proj,
    latter_factor_proj,
    outer_output_weight,
    pair_norm_gain,
    pair_logit_weight,
    content_vector_proj,
    sigmoid_switch_proj,
    final_result_proj,
    *,
    devs,
):
    seqs, toks, width = homolog_embedding.shape
    tokens = devs * toks
    heads = pair_logit_weight.shape[1]
    factor = former_factor_proj.shape[1]
    channels = outer_output_weight.shape[1]
    lanes = 2 * width
    half, outer = seqs // 2, seqs // 8
    params = pltpu.CompilerParams(vmem_limit_bytes=28 << 20)

    def keep(*arrays):
        return [pltpu.with_memory_space_constraint(a, pltpu.HBM) for a in arrays]

    def room(*arrays):
        return [pltpu.VMEM(a.shape, a.dtype) for a in arrays]

    arrays = (
        homolog_embedding,
        alignment_mask.T,
        lineup_standardize_scaling[None],
        token_real_mask[None],
    )
    packed = pl.pallas_call(
        pack_kernel,
        out_shape=jax.ShapeDtypeStruct((half + 1, toks, lanes), BF16),
        in_specs=[HB] * 4,
        out_specs=VM,
        scratch_shapes=room(*arrays) + [pltpu.SemaphoreType.DMA((4,))],
        compiler_params=params,
        name="pack",
    )(*keep(*arrays))

    def swap(block, shift):
        return lax.ppermute(block, "row", [(n, n ^ shift) for n in range(devs)])

    held = {0: packed}
    for shift in sorted(range(4, devs, 4), reverse=True):
        held[shift] = swap(packed, shift)
    for bit in (2, 1):
        for shift in sorted(held):
            held[shift ^ bit] = swap(held[shift], bit)
    shifts = tuple(sorted(held))

    arrays = (
        former_factor_proj.T,
        latter_factor_proj.T,
        outer_output_weight,
        content_vector_proj,
        sigmoid_switch_proj,
        final_result_proj.T,
    )
    folded, gate, right, value, result = pl.pallas_call(
        functools.partial(fold_kernel, seqs, heads),
        out_shape=(
            jax.ShapeDtypeStruct((toks // 2, outer, 8 * factor, 2 * channels), BF16),
            jax.ShapeDtypeStruct((heads // 2, half * toks, lanes), F32),
            jax.ShapeDtypeStruct((8 * width, 8 * factor), BF16),
            jax.ShapeDtypeStruct((heads // 2, 4 * width, lanes), BF16),
            jax.ShapeDtypeStruct((heads // 2, lanes, lanes), BF16),
        ),
        in_specs=[VM] + [HB] * 6,
        out_specs=(VM,) * 5,
        scratch_shapes=room(*arrays)
        + [
            pltpu.VMEM(outer_output_weight.shape, F32),
            pltpu.VMEM((seqs * toks, 128), F32),
            pltpu.VMEM((seqs * toks, factor), BF16),
            pltpu.SemaphoreType.DMA((6,)),
        ],
        compiler_params=params,
        cost_estimate=pl.CostEstimate(
            flops=10**9, bytes_accessed=10**7, transcendentals=10**6
        ),
        name="fold",
    )(packed, *keep(*arrays))
    arrays = (homolog_embedding, pair_state_tiles, pair_logit_weight.T, pair_norm_gain[None])
    out, pair = pl.pallas_call(
        functools.partial(main_kernel, seqs, heads, shifts),
        out_shape=(
            jax.ShapeDtypeStruct(homolog_embedding.shape, BF16),
            jax.ShapeDtypeStruct(pair_state_tiles.shape, BF16),
        ),
        in_specs=[VM] * devs + [HB] * 4 + [VM] * 5,
        out_specs=(VM, HB),
        scratch_shapes=room(*arrays)
        + [
            pltpu.VMEM(pair_state_tiles.shape, BF16),
            pltpu.VMEM((tokens, outer * 8 * factor), BF16),
            pltpu.VMEM((tokens, outer * 8 * factor), BF16),
            pltpu.VMEM((tokens // 128, heads * toks, 128), F32),
            pltpu.VMEM((half, heads * toks, lanes), BF16),
            pltpu.SemaphoreType.DMA((4,)),
            pltpu.SemaphoreType.DMA((toks,)),
        ],
        compiler_params=params,
        cost_estimate=pl.CostEstimate(flops=4 * 10**9, bytes_accessed=10**7, transcendentals=10**6),
        name="main",
    )(*[held[shift] for shift in shifts], *keep(*arrays), folded, gate, right, value, result)
    return out, pair


def solution(mesh):
    placed = (
        P("groups", "row", None),
        P(("groups", "row"), None, None),
        P("groups", "row"),
        P("groups"),
        P(),
        P(),
        P(),
        P(),
        P(),
        P(),
        P(),
        P(),
        P(),
    )
    devs = mesh.shape["row"]

    def body(*arrays):
        return shards(*arrays, devs=devs)

    return jax.shard_map(
        body,
        mesh=mesh,
        in_specs=placed,
        out_specs=(P("groups", "row", None), P(("groups", "row"), None, None)),
        check_vma=False,
    )
```

```python
import functools

import jax
import jax.numpy as jnp
from jax import lax
from jax.experimental import pallas as pl
from jax.experimental.pallas import tpu as pltpu
from jax.sharding import PartitionSpec as P


F32 = jnp.float32
BF16 = jnp.bfloat16
VM = pl.BlockSpec(memory_space=pltpu.VMEM)
UNROLL = 4
HB = pl.BlockSpec(memory_space=pltpu.HBM)


def dot(a, b):
    return jnp.dot(a, b, preferred_element_type=F32)


def dot_nt(a, b):
    return lax.dot_general(a, b, (((1,), (1,)), ((), ())), preferred_element_type=F32)


def iota(shape, axis):
    return lax.broadcasted_iota(jnp.int32, shape, axis)


def split(x):
    high = x.astype(BF16)
    return high, (x - high.astype(F32)).astype(BF16)


def twice(block):
    zero = jnp.zeros_like(block)
    return jnp.concatenate(
        [jnp.concatenate([block, zero], 1), jnp.concatenate([zero, block], 1)], 0
    )


def fetch(sources, targets, sems):
    copies = [pltpu.make_async_copy(a, b, sems.at[n]) for n, (a, b) in enumerate(zip(sources, targets))]
    for copy in copies:
        copy.start()
    return copies


def pack_kernel(rows_hbm, mask_hbm, gain_hbm, real_hbm, out_ref, rows_ref, mask_ref, gain_ref, real_ref, sems):
    copies = fetch(
        (rows_hbm, mask_hbm, gain_hbm, real_hbm), (rows_ref, mask_ref, gain_ref, real_ref), sems
    )
    for copy in copies:
        copy.wait()
    seqs, toks, width = rows_ref.shape
    outer = seqs // 8
    x = rows_ref[...].reshape(outer, 2, 4, toks, width)
    x = jnp.concatenate([x[:, 0], x[:, 1]], axis=-1).reshape(seqs // 2 * toks, 2 * width)
    lanes = 2 * width
    same = (iota((lanes, lanes), 0) // width) == (iota((lanes, lanes), 1) // width)
    mean_of = jnp.where(same, 1.0 / width, 0.0).astype(BF16)
    centered = x.astype(F32) - dot(x, mean_of)
    high, low = split(centered * centered)
    spread = dot(high, mean_of) + dot(low, mean_of)
    gain = jnp.concatenate([gain_ref[...], gain_ref[...]], axis=-1)
    normed = centered * lax.rsqrt(spread + 1e-05) * gain
    out_ref[: seqs // 2] = normed.astype(BF16).reshape(seqs // 2, toks, lanes)
    real = real_ref[...].astype(F32)
    tokens = real.shape[1]
    here = iota((toks, tokens), 1) == lax.axis_index("row") * toks + iota((toks, tokens), 0)
    mine = jnp.sum(jnp.where(here, real, 0.0), axis=1, keepdims=True)
    mask = mask_ref[...].astype(F32)
    mask = jnp.concatenate([mask, jnp.zeros((toks, lanes - seqs), F32)], axis=-1)
    mask = jnp.where(iota(mask.shape, 1) == seqs, mine, mask)
    out_ref[seqs // 2] = mask.astype(BF16)


def fold_kernel(
    seqs,
    heads,
    pack_ref,
    former_hbm,
    latter_hbm,
    outer_hbm,
    content_hbm,
    switch_hbm,
    final_hbm,
    folded_ref,
    gate_ref,
    right_ref,
    value_ref,
    result_ref,
    former_ref,
    latter_ref,
    outer_ref,
    content_ref,
    switch_ref,
    final_ref,
    weight_scr,
    left_scr,
    lhs_scr,
    sems,
):
    copies = fetch(
        (former_hbm, outer_hbm, latter_hbm, content_hbm, switch_hbm, final_hbm),
        (former_ref, outer_ref, latter_ref, content_ref, switch_ref, final_ref),
        sems,
    )
    half, toks, lanes = seqs // 2, pack_ref.shape[1], pack_ref.shape[2]
    factor, width = former_ref.shape
    outer = seqs // 8
    rows = pack_ref[:half].reshape(half * toks, lanes)
    copies[0].wait()
    left = dot_nt(rows, twice(former_ref[...]))
    for so in range(outer):
        for s2 in range(2):
            left_scr[pl.ds((so * 8 + s2 * 4) * toks, 4 * toks), :factor] = left[
                so * 4 * toks : (so + 1) * 4 * toks, s2 * factor : (s2 + 1) * factor
            ]
    eye = iota((seqs, seqs), 0) == iota((seqs, seqs), 1)
    mask = pack_ref[half].astype(F32)[:, :seqs]
    for i in range(toks):
        picked = jnp.where(eye, jnp.broadcast_to(mask[i : i + 1], (seqs, seqs)), 0.0)
        rows_i = left_scr[pl.ds(i, seqs, stride=toks), :][:, :factor].astype(BF16)
        lhs_scr[i * seqs : (i + 1) * seqs, :] = dot(picked.astype(BF16), rows_i).astype(BF16)
    copies[1].wait()
    weight_scr[...] = outer_ref[...].astype(F32)
    channels = outer_ref.shape[1]

    def step(m, carry):
        for u in range(UNROLL):
            e = 2 * (m * UNROLL + u)
            even = weight_scr[pl.ds(e, factor, stride=factor), :]
            odd = weight_scr[pl.ds(e + 1, factor, stride=factor), :]
            pair = jnp.concatenate([even, odd], axis=1).astype(BF16)
            product = dot(lhs_scr[...], pair)
            for i in range(toks):
                block = product[i * seqs : (i + 1) * seqs].reshape(outer, 8, 2 * channels)
                block = jnp.concatenate([block[:, :, :channels], block[:, :, channels:]], axis=1)
                first = i % 2 * channels
                folded_ref[
                    i // 2, :, pl.ds(pl.multiple_of(8 * e, 16), 16), first : first + channels
                ] = block.astype(BF16)
        return carry

    lax.fori_loop(0, factor // 2 // UNROLL, step, 0)
    for copy in copies[2:]:
        copy.wait()
    spread = jnp.where(
        iota((factor, 8 * factor), 0) == iota((factor, 8 * factor), 1) // 8, 1.0, 0.0
    ).astype(BF16)
    wide = dot(latter_ref[...].astype(F32).T.astype(BF16), spread)
    lane = iota(wide.shape, 1) % 8
    for rest in range(4):
        for s2 in range(2):
            base = (rest * 2 + s2) * width
            right_ref[base : base + width, :] = jnp.where(lane == s2 * 4 + rest, wide, 0.0).astype(
                BF16
            )
    column = content_ref.shape[1] // heads
    for hp in range(heads // 2):
        cols = slice(2 * column * hp, 2 * column * (hp + 1))
        gate_ref[hp] = jax.nn.sigmoid(dot(rows, twice(switch_ref[:, cols])))
        piece = content_ref[:, cols].astype(F32)
        which = iota(piece.shape, 1) // column
        zero = jnp.zeros_like(piece)
        for h2 in range(2):
            mine = jnp.where(which == h2, piece, 0.0)
            for s2 in range(2):
                base = (h2 * 2 + s2) * width
                row = [mine, zero] if s2 == 0 else [zero, mine]
                value_ref[hp, base : base + width, :] = jnp.concatenate(row, 1).astype(BF16)
        result_ref[hp] = twice(final_ref[:, cols])


def main_kernel(seqs, heads, shifts, *refs):
    blocks = refs[: len(shifts)]
    (
        rows_hbm,
        state_hbm,
        weight_hbm,
        gain_hbm,
        folded_ref,
        gate_ref,
        right_ref,
        value_ref,
        result_ref,
        out_ref,
        pair_hbm,
        rows_ref,
        state_ref,
        weight_ref,
        gain_ref,
        pair_ref,
        wide_scr,
        rhs_scr,
        logits_scr,
        mixed_scr,
        inverse_scr,
        lhs_scr,
        even_scr,
        odd_scr,
        both_scr,
        sems,
        pair_sem,
    ) = refs[len(shifts) :]
    copies = fetch(
        (weight_hbm, gain_hbm, state_hbm, rows_hbm),
        (weight_ref, gain_ref, state_ref, rows_ref),
        sems,
    )
    half = seqs // 2
    outer = seqs // 8
    devs = len(shifts)
    _, toks, lanes = blocks[0].shape
    tokens = devs * toks
    me = lax.axis_index("row")

    def place(shift):
        where = 0
        bit = 1
        while bit < devs:
            mine = (me // bit) % 2
            where = where + bit * ((1 - mine) if shift & bit else mine)
            bit *= 2
        return pl.multiple_of(where * toks, toks)

    spots = [place(k) for k in shifts]

    def gathered(n):
        return jnp.concatenate([block[n] for block in blocks], axis=0)

    mask = gathered(half)
    inverse = 1.0 / (1.0 + dot_nt(mask, jnp.where(iota((toks, lanes), 1) < seqs, blocks[0][half], 0)))
    real = dot_nt(jnp.where(iota((8, lanes), 1) == seqs, 1.0, 0.0).astype(BF16), mask)
    wide = right_ref.shape[1]
    which = iota((lanes, wide), 0) - iota((lanes, wide), 1) % 8
    for so in range(outer):
        pick = jnp.where(which == 8 * so, 1.0, 0.0).astype(BF16)
        wide_scr[:, so * wide : (so + 1) * wide] = dot(mask, pick).astype(BF16)
    for i in range(toks):
        inverse_scr[i] = jnp.broadcast_to(inverse[:, i : i + 1], inverse_scr.shape[1:])
    for so in range(outer):
        rows = jnp.concatenate([gathered(so * 4 + r) for r in range(4)], axis=1)
        cols = slice(so * wide, (so + 1) * wide)
        rhs_scr[:, cols] = (dot(rows, right_ref[...]) * wide_scr[:, cols].astype(F32)).astype(BF16)
    for copy in copies:
        copy.wait()
    w_high, w_low = split(weight_ref[...] * gain_ref[...])
    lhs_scr[...] = jnp.concatenate(
        [
            jnp.concatenate([w_high, w_high], axis=1),
            jnp.concatenate([w_low, jnp.zeros_like(w_low)], axis=1),
        ],
        axis=0,
    )
    channels = state_ref.shape[-1]

    def product(ip, acc_scr):
        acc_scr[...] = dot(rhs_scr[...], folded_ref[ip].reshape(outer * wide, 2 * channels))

    def finish(ip, acc_scr):
        for i2 in range(2):
            i = 2 * ip + i2
            for n, spot in enumerate(spots):
                here = slice(n * toks, (n + 1) * toks)
                x = state_ref[i, pl.ds(spot, toks), :].astype(F32) + (
                    acc_scr[here, i2 * channels : (i2 + 1) * channels] * inverse_scr[i, here, :]
                )
                x = x.astype(BF16)
                pair_ref[i, pl.ds(spot, toks), :] = x
                x = x.astype(F32)
                x = x - jnp.mean(x, axis=-1, keepdims=True)
                spread = jnp.mean(x * x, axis=-1, keepdims=True)
                high, low = split(x * lax.rsqrt(spread + 1e-05))
                both_scr[i2, here, :channels] = high
                both_scr[i2, here, channels:] = low
            pltpu.make_async_copy(pair_ref.at[i], pair_hbm.at[i], pair_sem.at[i]).start()
            logits = dot_nt(lhs_scr[...], both_scr[i2])
            logits = logits[:heads] + logits[heads:]
            for jb in range(tokens // 128):
                logits_scr[jb, pl.ds(i, heads, stride=toks), :] = logits[
                    :, jb * 128 : jb * 128 + 128
                ]

    product(0, even_scr)
    for ip in range(toks // 2):
        if ip + 1 < toks // 2:
            product(ip + 1, odd_scr if ip % 2 == 0 else even_scr)
        finish(ip, even_scr if ip % 2 == 0 else odd_scr)
    logits = jnp.concatenate([logits_scr[jb] for jb in range(tokens // 128)], axis=1)
    logits = jnp.where(real[:1] > 0.5, logits, -1000000000.0)
    top = jnp.max(logits, axis=-1, keepdims=True)
    power = jnp.exp(logits - top)
    probs = (power / jnp.sum(power, axis=-1, keepdims=True)).astype(BF16)
    for b in range(0, half, 2):
        mixed = dot(probs, jnp.concatenate([gathered(b), gathered(b + 1)], axis=1)).astype(BF16)
        mixed_scr[b] = mixed[:, :lanes]
        mixed_scr[b + 1] = mixed[:, lanes:]
    total = None
    for hp in range(heads // 2):
        pair = jnp.concatenate(
            [
                mixed_scr[:, (2 * hp + h2) * toks : (2 * hp + h2 + 1) * toks, :].reshape(
                    half * toks, lanes
                )
                for h2 in range(2)
            ],
            axis=1,
        )
        average = dot(pair, value_ref[hp])
        gated = (gate_ref[hp] * average).astype(BF16)
        part = dot_nt(gated, result_ref[hp])
        total = part if total is None else total + part
    width = rows_ref.shape[2]
    total = total.reshape(outer, 4, toks, lanes)
    base = rows_ref[...].astype(F32).reshape(outer, 2, 4, toks, width)
    for s2 in range(2):
        piece = base[:, s2] + total[..., s2 * width : (s2 + 1) * width]
        for so in range(outer):
            out_ref[so * 8 + s2 * 4 : so * 8 + s2 * 4 + 4] = piece[so].astype(BF16)
    for i in range(toks):
        pltpu.make_async_copy(pair_ref.at[i], pair_hbm.at[i], pair_sem.at[i]).wait()


def far_order(devs):
    far = list(range(4, devs, 4))
    return far[:1] + far[:0:-1]


def shards(
    homolog_embedding,
    pair_state_tiles,
    alignment_mask,
    token_real_mask,
    lineup_standardize_scaling,
    former_factor_proj,
    latter_factor_proj,
    outer_output_weight,
    pair_norm_gain,
    pair_logit_weight,
    content_vector_proj,
    sigmoid_switch_proj,
    final_result_proj,
    *,
    devs,
):
    seqs, toks, width = homolog_embedding.shape
    tokens = devs * toks
    heads = pair_logit_weight.shape[1]
    factor = former_factor_proj.shape[1]
    channels = outer_output_weight.shape[1]
    lanes = 2 * width
    half, outer = seqs // 2, seqs // 8
    params = pltpu.CompilerParams(vmem_limit_bytes=28 << 20)

    def keep(*arrays):
        return [pltpu.with_memory_space_constraint(a, pltpu.HBM) for a in arrays]

    def room(*arrays):
        return [pltpu.VMEM(a.shape, a.dtype) for a in arrays]

    arrays = (
        homolog_embedding,
        alignment_mask.T,
        lineup_standardize_scaling[None],
        token_real_mask[None],
    )
    packed = pl.pallas_call(
        pack_kernel,
        out_shape=jax.ShapeDtypeStruct((half + 1, toks, lanes), BF16),
        in_specs=[HB] * 4,
        out_specs=VM,
        scratch_shapes=room(*arrays) + [pltpu.SemaphoreType.DMA((4,))],
        compiler_params=params,
        name="pack",
    )(*keep(*arrays))

    def swap(block, shift):
        return lax.ppermute(block, "row", [(n, n ^ shift) for n in range(devs)])

    held = {0: packed}
    far = far_order(devs)
    for shift in far:
        held[shift] = swap(packed, shift)
    for bit in (2, 1):
        for shift in list(held):
            held[shift ^ bit] = swap(held[shift], bit)
    shifts = tuple(sorted(held))

    arrays = (
        former_factor_proj.T,
        latter_factor_proj.T,
        outer_output_weight,
        content_vector_proj,
        sigmoid_switch_proj,
        final_result_proj.T,
    )
    folded, gate, right, value, result = pl.pallas_call(
        functools.partial(fold_kernel, seqs, heads),
        out_shape=(
            jax.ShapeDtypeStruct((toks // 2, outer, 8 * factor, 2 * channels), BF16),
            jax.ShapeDtypeStruct((heads // 2, half * toks, lanes), F32),
            jax.ShapeDtypeStruct((8 * width, 8 * factor), BF16),
            jax.ShapeDtypeStruct((heads // 2, 4 * width, lanes), BF16),
            jax.ShapeDtypeStruct((heads // 2, lanes, lanes), BF16),
        ),
        in_specs=[VM] + [HB] * 6,
        out_specs=(VM,) * 5,
        scratch_shapes=room(*arrays)
        + [
            pltpu.VMEM(outer_output_weight.shape, F32),
            pltpu.VMEM((seqs * toks, 128), F32),
            pltpu.VMEM((seqs * toks, factor), BF16),
            pltpu.SemaphoreType.DMA((6,)),
        ],
        compiler_params=params,
        cost_estimate=pl.CostEstimate(
            flops=10**9, bytes_accessed=10**7, transcendentals=10**6
        ),
        name="fold",
    )(packed, *keep(*arrays))
    arrays = (homolog_embedding, pair_state_tiles, pair_logit_weight.T, pair_norm_gain[None])
    out, pair = pl.pallas_call(
        functools.partial(main_kernel, seqs, heads, shifts),
        out_shape=(
            jax.ShapeDtypeStruct(homolog_embedding.shape, BF16),
            jax.ShapeDtypeStruct(pair_state_tiles.shape, BF16),
        ),
        in_specs=[VM] * devs + [HB] * 4 + [VM] * 5,
        out_specs=(VM, HB),
        scratch_shapes=room(*arrays)
        + [
            pltpu.VMEM(pair_state_tiles.shape, BF16),
            pltpu.VMEM((tokens, outer * 8 * factor), BF16),
            pltpu.VMEM((tokens, outer * 8 * factor), BF16),
            pltpu.VMEM((tokens // 128, heads * toks, 128), F32),
            pltpu.VMEM((half, heads * toks, lanes), BF16),
            pltpu.VMEM((toks, tokens, channels), F32),
            pltpu.VMEM((2 * heads, 2 * channels), BF16),
            pltpu.VMEM((tokens, 2 * channels), F32),
            pltpu.VMEM((tokens, 2 * channels), F32),
            pltpu.VMEM((2, tokens, 2 * channels), BF16),
            pltpu.SemaphoreType.DMA((4,)),
            pltpu.SemaphoreType.DMA((toks,)),
        ],
        compiler_params=params,
        cost_estimate=pl.CostEstimate(flops=4 * 10**9, bytes_accessed=10**7, transcendentals=10**6),
        name="main",
    )(*[held[shift] for shift in shifts], *keep(*arrays), folded, gate, right, value, result)
    return out, pair


def solution(mesh):
    placed = (
        P("groups", "row", None),
        P(("groups", "row"), None, None),
        P("groups", "row"),
        P("groups"),
        P(),
        P(),
        P(),
        P(),
        P(),
        P(),
        P(),
        P(),
        P(),
    )
    devs = mesh.shape["row"]

    def body(*arrays):
        return shards(*arrays, devs=devs)

    return jax.shard_map(
        body,
        mesh=mesh,
        in_specs=placed,
        out_specs=(P("groups", "row", None), P(("groups", "row"), None, None)),
        check_vma=False,
    )
```

```python
import functools

import jax
import jax.numpy as jnp
from jax import lax
from jax.experimental import pallas as pl
from jax.experimental.pallas import tpu as pltpu
from jax.sharding import PartitionSpec as P


F32 = jnp.float32
BF16 = jnp.bfloat16
VM = pl.BlockSpec(memory_space=pltpu.VMEM)
GROUP = 4
HB = pl.BlockSpec(memory_space=pltpu.HBM)


def dot(a, b):
    return jnp.dot(a, b, preferred_element_type=F32)


def dot_nt(a, b):
    return lax.dot_general(a, b, (((1,), (1,)), ((), ())), preferred_element_type=F32)


def iota(shape, axis):
    return lax.broadcasted_iota(jnp.int32, shape, axis)


def split(x):
    high = x.astype(BF16)
    return high, (x - high.astype(F32)).astype(BF16)


def twice(block):
    zero = jnp.zeros_like(block)
    return jnp.concatenate(
        [jnp.concatenate([block, zero], 1), jnp.concatenate([zero, block], 1)], 0
    )


def fetch(sources, targets, sems):
    copies = [pltpu.make_async_copy(a, b, sems.at[n]) for n, (a, b) in enumerate(zip(sources, targets))]
    for copy in copies:
        copy.start()
    return copies


def pack_kernel(rows_hbm, mask_hbm, gain_hbm, real_hbm, out_ref, rows_ref, mask_ref, gain_ref, real_ref, sems):
    copies = fetch(
        (rows_hbm, mask_hbm, gain_hbm, real_hbm), (rows_ref, mask_ref, gain_ref, real_ref), sems
    )
    for copy in copies:
        copy.wait()
    seqs, toks, width = rows_ref.shape
    outer = seqs // 8
    x = rows_ref[...].reshape(outer, 2, 4, toks, width)
    x = jnp.concatenate([x[:, 0], x[:, 1]], axis=-1).reshape(seqs // 2 * toks, 2 * width)
    lanes = 2 * width
    same = (iota((lanes, lanes), 0) // width) == (iota((lanes, lanes), 1) // width)
    mean_of = jnp.where(same, 1.0 / width, 0.0).astype(BF16)
    centered = x.astype(F32) - dot(x, mean_of)
    high, low = split(centered * centered)
    spread = dot(high, mean_of) + dot(low, mean_of)
    gain = jnp.concatenate([gain_ref[...], gain_ref[...]], axis=-1)
    normed = centered * lax.rsqrt(spread + 1e-05) * gain
    out_ref[: seqs // 2] = normed.astype(BF16).reshape(seqs // 2, toks, lanes)
    real = real_ref[...].astype(F32)
    tokens = real.shape[1]
    here = iota((toks, tokens), 1) == lax.axis_index("row") * toks + iota((toks, tokens), 0)
    mine = jnp.sum(jnp.where(here, real, 0.0), axis=1, keepdims=True)
    mask = mask_ref[...].astype(F32)
    mask = jnp.concatenate([mask, jnp.zeros((toks, lanes - seqs), F32)], axis=-1)
    mask = jnp.where(iota(mask.shape, 1) == seqs, mine, mask)
    out_ref[seqs // 2] = mask.astype(BF16)


def positions(devs, toks, shifts):
    me = lax.axis_index("row")
    spots = []
    for shift in shifts:
        where = 0
        bit = 1
        while bit < devs:
            mine = (me // bit) % 2
            where = where + bit * ((1 - mine) if shift & bit else mine)
            bit *= 2
        spots.append(pl.multiple_of(where * toks, toks))
    return spots


def turn_kernel(shifts, state_hbm, turned_ref, state_ref, sems):
    toks = state_ref.shape[0]
    copies = [
        pltpu.make_async_copy(state_hbm.at[i], state_ref.at[i], sems.at[i]) for i in range(toks)
    ]
    for copy in copies:
        copy.start()
    spots = positions(len(shifts), toks, shifts)
    group = 128 // toks
    for i in range(toks):
        copies[i].wait()
        for jb in range(len(shifts) // group):
            rows = [
                state_ref[i, pl.ds(spot, toks), :] for spot in spots[jb * group : (jb + 1) * group]
            ]
            block = jnp.concatenate(rows, axis=0).astype(F32).T
            turned_ref[i, :, jb * 128 : (jb + 1) * 128] = block.astype(BF16)


def fold_kernel(
    seqs,
    heads,
    pack_ref,
    former_hbm,
    outer_hbm,
    latter_hbm,
    content_hbm,
    switch_hbm,
    final_hbm,
    folded_ref,
    gate_ref,
    right_ref,
    value_ref,
    result_ref,
    former_ref,
    outer_ref,
    latter_ref,
    content_ref,
    switch_ref,
    final_ref,
    weight_scr,
    left_scr,
    lhs_scr,
    rhs_scr,
    sems,
):
    copies = fetch(
        (former_hbm, outer_hbm, latter_hbm, content_hbm, switch_hbm, final_hbm),
        (former_ref, outer_ref, latter_ref, content_ref, switch_ref, final_ref),
        sems,
    )
    half, toks, lanes = seqs // 2, pack_ref.shape[1], pack_ref.shape[2]
    factor, width = former_ref.shape
    outer = seqs // 8
    rows = pack_ref[:half].reshape(half * toks, lanes)
    copies[0].wait()
    left = dot_nt(rows, twice(former_ref[...]))
    for so in range(outer):
        for s2 in range(2):
            left_scr[pl.ds((so * 8 + s2 * 4) * toks, 4 * toks), :factor] = left[
                so * 4 * toks : (so + 1) * 4 * toks, s2 * factor : (s2 + 1) * factor
            ]
    eye = iota((seqs, seqs), 0) == iota((seqs, seqs), 1)
    mask = pack_ref[half].astype(F32)[:, :seqs]
    for i in range(toks):
        picked = jnp.where(eye, jnp.broadcast_to(mask[i : i + 1], (seqs, seqs)), 0.0)
        rows_i = left_scr[pl.ds(i, seqs, stride=toks), :][:, :factor].T.astype(BF16)
        rhs_scr[i // 2, :, i % 2 * 2 * seqs : (i % 2 + 1) * 2 * seqs] = twice(
            dot(rows_i, picked.astype(BF16))
        ).astype(BF16)
    copies[1].wait()
    weight_scr[...] = outer_ref[...].astype(F32)
    channels = outer_ref.shape[1]
    for ep in range(factor // 2):
        even = weight_scr[pl.ds(2 * ep, factor, stride=factor), :]
        odd = weight_scr[pl.ds(2 * ep + 1, factor, stride=factor), :]
        lhs_scr[ep * channels : (ep + 1) * channels, :] = jnp.concatenate(
            [even, odd], axis=0
        ).T.astype(BF16)

    def step(ip, carry):
        product = dot(lhs_scr[...], rhs_scr[ip]).astype(BF16)
        for ep in range(factor // 2):
            for i2 in range(2):
                folded_ref[2 * ip + i2, :, ep * 2 * seqs : (ep + 1) * 2 * seqs] = product[
                    ep * channels : (ep + 1) * channels, i2 * 2 * seqs : (i2 + 1) * 2 * seqs
                ]
        return carry

    lax.fori_loop(0, toks // 2, step, 0)
    for copy in copies[2:]:
        copy.wait()
    spread = jnp.where(
        iota((8 * factor, factor), 0) // 8 == iota((8 * factor, factor), 1), 1.0, 0.0
    ).astype(BF16)
    tall = dot(spread, latter_ref[...])
    row = iota(tall.shape, 0) % 8
    right_ref[...] = jnp.concatenate(
        [jnp.where(row == s2 * 4 + rest, tall, 0.0) for rest in range(4) for s2 in range(2)], axis=1
    ).astype(BF16)
    column = content_ref.shape[1] // heads
    for hp in range(heads // 2):
        cols = slice(2 * column * hp, 2 * column * (hp + 1))
        gate_ref[hp] = jax.nn.sigmoid(dot(rows, twice(switch_ref[:, cols])))
        piece = content_ref[:, cols].astype(F32)
        which = iota(piece.shape, 1) // column
        zero = jnp.zeros_like(piece)
        for h2 in range(2):
            mine = jnp.where(which == h2, piece, 0.0)
            for s2 in range(2):
                base = (h2 * 2 + s2) * width
                row = [mine, zero] if s2 == 0 else [zero, mine]
                value_ref[hp, base : base + width, :] = jnp.concatenate(row, 1).astype(BF16)
        result_ref[hp] = twice(final_ref[:, cols])


def main_kernel(seqs, heads, shifts, *refs):
    blocks = refs[: len(shifts)]
    (
        rows_hbm,
        weight_hbm,
        gain_hbm,
        turned_ref,
        folded_ref,
        gate_ref,
        right_ref,
        value_ref,
        result_ref,
        out_ref,
        pair_hbm,
        rows_ref,
        weight_ref,
        gain_ref,
        pair_ref,
        mask_scr,
        rhs_scr,
        logits_scr,
        mixed_scr,
        even_scr,
        odd_scr,
        sems,
        pair_sem,
    ) = refs[len(shifts) :]
    copies = fetch(
        (weight_hbm, gain_hbm, rows_hbm),
        (weight_ref, gain_ref, rows_ref),
        sems,
    )
    half = seqs // 2
    outer = seqs // 8
    devs = len(shifts)
    _, toks, lanes = blocks[0].shape
    tokens = devs * toks
    tiles = tokens // 128
    spots = positions(devs, toks, shifts)

    def gathered(n):
        return jnp.concatenate([block[n] for block in blocks], axis=0)

    mask = gathered(half)
    own = jnp.where(iota((toks, lanes), 1) < seqs, blocks[0][half], 0)
    inverse = 1.0 / (1.0 + dot_nt(own, mask))
    pick = jnp.where(iota((seqs + 8, lanes), 0) == iota((seqs + 8, lanes), 1), 1.0, 0.0)
    mask_scr[...] = dot_nt(pick.astype(BF16), mask)
    real = mask_scr[seqs : seqs + 1, :]
    factor = rhs_scr.shape[0]
    for so in range(0, outer, 2):
        pieces = []
        for n in (so, so + 1):
            rows = jnp.concatenate([gathered(n * 4 + r) for r in range(4)], axis=1)
            right = dot_nt(right_ref[...], rows).reshape(factor, 8, tokens)
            pieces.append(right * mask_scr[n * 8 : n * 8 + 8, :])
        rhs_scr[:, so * 8 : so * 8 + 16, :] = jnp.concatenate(pieces, axis=1).astype(BF16)
    for copy in copies[:2]:
        copy.wait()
    w_high, w_low = split(weight_ref[...] * gain_ref[...])
    weights = jnp.concatenate([w_high, w_low], axis=0)
    w_sum = jnp.sum(w_high.astype(F32) + w_low.astype(F32), axis=1, keepdims=True)
    channels = turned_ref.shape[1]
    group = even_scr.shape[0] // channels

    def product(g, acc_scr):
        rows = folded_ref[g * group : (g + 1) * group].reshape(group * channels, -1)
        acc_scr[...] = dot(rows, rhs_scr[...].reshape(factor * seqs, tokens))

    def finish(g, acc_scr):
        for n in range(group):
            i = g * group + n
            for jb in range(tiles):
                cols = slice(jb * 128, (jb + 1) * 128)
                update = acc_scr[n * channels : (n + 1) * channels, cols] * inverse[i : i + 1, cols]
                x = (turned_ref[i, :, cols].astype(F32) + update).astype(BF16)
                logits = dot(weights, x)
                x = x.astype(F32)
                turned = x.T.astype(BF16)
                for k in range(128 // toks):
                    spot = spots[jb * (128 // toks) + k]
                    pair_ref[i, pl.ds(spot, toks), :] = turned[k * toks : (k + 1) * toks]
                mean = jnp.mean(x, axis=0, keepdims=True)
                x = x - mean
                scale = lax.rsqrt(jnp.mean(x * x, axis=0, keepdims=True) + 1e-05)
                logits = (logits[:heads] + logits[heads:] - w_sum * mean) * scale
                logits_scr[jb, pl.ds(i, heads, stride=toks), :] = logits
            pltpu.make_async_copy(pair_ref.at[i], pair_hbm.at[i], pair_sem.at[i]).start()

    scratch = (even_scr, odd_scr)
    product(0, even_scr)
    for g in range(toks // group):
        if g + 1 < toks // group:
            product(g + 1, scratch[(g + 1) % 2])
        finish(g, scratch[g % 2])
    logits = jnp.concatenate([logits_scr[jb] for jb in range(tiles)], axis=1)
    logits = jnp.where(real > 0.5, logits, -1000000000.0)
    top = jnp.max(logits, axis=-1, keepdims=True)
    power = jnp.exp(logits - top)
    probs = (power / jnp.sum(power, axis=-1, keepdims=True)).astype(BF16)
    for b in range(0, half, 2):
        mixed = dot(probs, jnp.concatenate([gathered(b), gathered(b + 1)], axis=1)).astype(BF16)
        mixed_scr[b] = mixed[:, :lanes]
        mixed_scr[b + 1] = mixed[:, lanes:]
    total = None
    for hp in range(heads // 2):
        pair = jnp.concatenate(
            [
                mixed_scr[:, (2 * hp + h2) * toks : (2 * hp + h2 + 1) * toks, :].reshape(
                    half * toks, lanes
                )
                for h2 in range(2)
            ],
            axis=1,
        )
        average = dot(pair, value_ref[hp])
        gated = (gate_ref[hp] * average).astype(BF16)
        part = dot_nt(gated, result_ref[hp])
        total = part if total is None else total + part
    copies[2].wait()
    width = rows_ref.shape[2]
    total = total.reshape(outer, 4, toks, lanes)
    base = rows_ref[...].astype(F32).reshape(outer, 2, 4, toks, width)
    for s2 in range(2):
        piece = base[:, s2] + total[..., s2 * width : (s2 + 1) * width]
        for so in range(outer):
            out_ref[so * 8 + s2 * 4 : so * 8 + s2 * 4 + 4] = piece[so].astype(BF16)
    for i in range(toks):
        pltpu.make_async_copy(pair_ref.at[i], pair_hbm.at[i], pair_sem.at[i]).wait()


def far_order(devs):
    far = list(range(4, devs, 4))
    return far[:1] + far[:0:-1]


def shards(
    homolog_embedding,
    pair_state_tiles,
    alignment_mask,
    token_real_mask,
    lineup_standardize_scaling,
    former_factor_proj,
    latter_factor_proj,
    outer_output_weight,
    pair_norm_gain,
    pair_logit_weight,
    content_vector_proj,
    sigmoid_switch_proj,
    final_result_proj,
    *,
    devs,
):
    seqs, toks, width = homolog_embedding.shape
    tokens = devs * toks
    heads = pair_logit_weight.shape[1]
    factor = former_factor_proj.shape[1]
    channels = outer_output_weight.shape[1]
    lanes = 2 * width
    half = seqs // 2
    params = pltpu.CompilerParams(vmem_limit_bytes=28 << 20)

    def keep(*arrays):
        return [pltpu.with_memory_space_constraint(a, pltpu.HBM) for a in arrays]

    def room(*arrays):
        return [pltpu.VMEM(a.shape, a.dtype) for a in arrays]

    arrays = (
        homolog_embedding,
        alignment_mask.T,
        lineup_standardize_scaling[None],
        token_real_mask[None],
    )
    packed = pl.pallas_call(
        pack_kernel,
        out_shape=jax.ShapeDtypeStruct((half + 1, toks, lanes), BF16),
        in_specs=[HB] * 4,
        out_specs=VM,
        scratch_shapes=room(*arrays) + [pltpu.SemaphoreType.DMA((4,))],
        compiler_params=params,
        name="pack",
    )(*keep(*arrays))

    def swap(block, shift):
        return lax.ppermute(block, "row", [(n, n ^ shift) for n in range(devs)])

    held = {0: packed}
    far = far_order(devs)
    for shift in far:
        held[shift] = swap(packed, shift)
    for bit in (2, 1):
        for shift in list(held):
            held[shift ^ bit] = swap(held[shift], bit)
    shifts = tuple(sorted(held))

    arrays = (
        former_factor_proj.T,
        outer_output_weight,
        latter_factor_proj.T,
        content_vector_proj,
        sigmoid_switch_proj,
        final_result_proj.T,
    )
    folded, gate, right, value, result = pl.pallas_call(
        functools.partial(fold_kernel, seqs, heads),
        out_shape=(
            jax.ShapeDtypeStruct((toks, channels, factor * seqs), BF16),
            jax.ShapeDtypeStruct((heads // 2, half * toks, lanes), F32),
            jax.ShapeDtypeStruct((8 * factor, 8 * width), BF16),
            jax.ShapeDtypeStruct((heads // 2, 4 * width, lanes), BF16),
            jax.ShapeDtypeStruct((heads // 2, lanes, lanes), BF16),
        ),
        in_specs=[VM] + [HB] * 6,
        out_specs=(VM,) * 5,
        scratch_shapes=room(*arrays)
        + [
            pltpu.VMEM(outer_output_weight.shape, F32),
            pltpu.VMEM((seqs * toks, 128), F32),
            pltpu.VMEM((factor // 2 * channels, 2 * factor), BF16),
            pltpu.VMEM((toks // 2, 2 * factor, 4 * seqs), BF16),
            pltpu.SemaphoreType.DMA((6,)),
        ],
        compiler_params=params,
        cost_estimate=pl.CostEstimate(
            flops=10**9, bytes_accessed=10**7, transcendentals=10**6
        ),
        name="fold",
    )(packed, *keep(*arrays))
    turned = pl.pallas_call(
        functools.partial(turn_kernel, shifts),
        out_shape=jax.ShapeDtypeStruct((toks, channels, tokens), BF16),
        in_specs=[HB],
        out_specs=VM,
        scratch_shapes=room(pair_state_tiles) + [pltpu.SemaphoreType.DMA((toks,))],
        compiler_params=params,
        cost_estimate=pl.CostEstimate(flops=10**7, bytes_accessed=10**6, transcendentals=0),
        name="turn",
    )(*keep(pair_state_tiles))
    arrays = (homolog_embedding, pair_logit_weight.T, pair_norm_gain[None])
    group = GROUP
    out, pair = pl.pallas_call(
        functools.partial(main_kernel, seqs, heads, shifts),
        out_shape=(
            jax.ShapeDtypeStruct(homolog_embedding.shape, BF16),
            jax.ShapeDtypeStruct(pair_state_tiles.shape, BF16),
        ),
        in_specs=[VM] * devs + [HB] * 3 + [VM] * 6,
        out_specs=(VM, HB),
        scratch_shapes=room(*arrays)
        + [
            pltpu.VMEM(pair_state_tiles.shape, BF16),
            pltpu.VMEM((seqs + 8, tokens), F32),
            pltpu.VMEM((factor, seqs, tokens), BF16),
            pltpu.VMEM((tokens // 128, heads * toks, 128), F32),
            pltpu.VMEM((half, heads * toks, lanes), BF16),
            pltpu.VMEM((group * channels, tokens), F32),
            pltpu.VMEM((group * channels, tokens), F32),
            pltpu.SemaphoreType.DMA((3,)),
            pltpu.SemaphoreType.DMA((toks,)),
        ],
        compiler_params=params,
        cost_estimate=pl.CostEstimate(flops=4 * 10**9, bytes_accessed=10**7, transcendentals=10**6),
        name="main",
    )(
        *[held[shift] for shift in shifts],
        *keep(*arrays),
        turned,
        folded,
        gate,
        right,
        value,
        result,
    )
    return out, pair


def solution(mesh):
    placed = (
        P("groups", "row", None),
        P(("groups", "row"), None, None),
        P("groups", "row"),
        P("groups"),
        P(),
        P(),
        P(),
        P(),
        P(),
        P(),
        P(),
        P(),
        P(),
    )
    devs = mesh.shape["row"]

    def body(*arrays):
        return shards(*arrays, devs=devs)

    return jax.shard_map(
        body,
        mesh=mesh,
        in_specs=placed,
        out_specs=(P("groups", "row", None), P(("groups", "row"), None, None)),
        check_vma=False,
    )
```

```python
import functools

import jax
import jax.numpy as jnp
from jax import lax
from jax.experimental import pallas as pl
from jax.experimental.pallas import tpu as pltpu
from jax.sharding import PartitionSpec as P


F32 = jnp.float32
BF16 = jnp.bfloat16
VM = pl.BlockSpec(memory_space=pltpu.VMEM)
GROUP = 4
HB = pl.BlockSpec(memory_space=pltpu.HBM)


def dot(a, b):
    return jnp.dot(a, b, preferred_element_type=F32)


def dot_nt(a, b):
    return lax.dot_general(a, b, (((1,), (1,)), ((), ())), preferred_element_type=F32)


def iota(shape, axis):
    return lax.broadcasted_iota(jnp.int32, shape, axis)


def split(x):
    high = x.astype(BF16)
    return high, (x - high.astype(F32)).astype(BF16)


def twice(block):
    zero = jnp.zeros_like(block)
    return jnp.concatenate(
        [jnp.concatenate([block, zero], 1), jnp.concatenate([zero, block], 1)], 0
    )


def fetch(sources, targets, sems):
    copies = [pltpu.make_async_copy(a, b, sems.at[n]) for n, (a, b) in enumerate(zip(sources, targets))]
    for copy in copies:
        copy.start()
    return copies


def pack_kernel(
    rows_hbm,
    mask_hbm,
    gain_hbm,
    real_hbm,
    former_hbm,
    out_ref,
    former_ref,
    rows_ref,
    mask_ref,
    gain_ref,
    real_ref,
    sems,
):
    copies = fetch(
        (rows_hbm, mask_hbm, gain_hbm, real_hbm, former_hbm),
        (rows_ref, mask_ref, gain_ref, real_ref, former_ref),
        sems,
    )
    for copy in copies:
        copy.wait()
    seqs, toks, width = rows_ref.shape
    outer = seqs // 8
    x = rows_ref[...].reshape(outer, 2, 4, toks, width)
    x = jnp.concatenate([x[:, 0], x[:, 1]], axis=-1).reshape(seqs // 2 * toks, 2 * width)
    lanes = 2 * width
    same = (iota((lanes, lanes), 0) // width) == (iota((lanes, lanes), 1) // width)
    mean_of = jnp.where(same, 1.0 / width, 0.0).astype(BF16)
    centered = x.astype(F32) - dot(x, mean_of)
    high, low = split(centered * centered)
    spread = dot(high, mean_of) + dot(low, mean_of)
    gain = jnp.concatenate([gain_ref[...], gain_ref[...]], axis=-1)
    normed = centered * lax.rsqrt(spread + 1e-05) * gain
    out_ref[: seqs // 2] = normed.astype(BF16).reshape(seqs // 2, toks, lanes)
    real = real_ref[...].astype(F32)
    tokens = real.shape[1]
    here = iota((toks, tokens), 1) == lax.axis_index("row") * toks + iota((toks, tokens), 0)
    mine = jnp.sum(jnp.where(here, real, 0.0), axis=1, keepdims=True)
    mask = mask_ref[...].astype(F32)
    mask = jnp.concatenate([mask, jnp.zeros((toks, lanes - seqs), F32)], axis=-1)
    mask = jnp.where(iota(mask.shape, 1) == seqs, mine, mask)
    out_ref[seqs // 2] = mask.astype(BF16)


def positions(devs, toks, shifts):
    me = lax.axis_index("row")
    spots = []
    for shift in shifts:
        where = 0
        bit = 1
        while bit < devs:
            mine = (me // bit) % 2
            where = where + bit * ((1 - mine) if shift & bit else mine)
            bit *= 2
        spots.append(pl.multiple_of(where * toks, toks))
    return spots


def turn_kernel(shifts, state_ref, turned_ref):
    toks = state_ref.shape[0]
    spots = positions(len(shifts), toks, shifts)
    group = 128 // toks
    for i in range(toks):
        for jb in range(len(shifts) // group):
            rows = [
                state_ref[i, pl.ds(spot, toks), :] for spot in spots[jb * group : (jb + 1) * group]
            ]
            block = jnp.concatenate(rows, axis=0).astype(F32).T
            turned_ref[i, :, jb * 128 : (jb + 1) * 128] = block.astype(BF16)


def fold_kernel(
    seqs,
    pack_ref,
    former_ref,
    outer_hbm,
    state_hbm,
    folded_ref,
    state_ref,
    outer_ref,
    weight_scr,
    left_scr,
    lhs_scr,
    rhs_scr,
    sems,
):
    copies = fetch((outer_hbm, state_hbm), (outer_ref, state_ref), sems)
    half, toks, lanes = seqs // 2, pack_ref.shape[1], pack_ref.shape[2]
    factor, _ = former_ref.shape
    outer = seqs // 8
    rows = pack_ref[:half].reshape(half * toks, lanes)
    left = dot_nt(rows, twice(former_ref[...]))
    for so in range(outer):
        for s2 in range(2):
            left_scr[pl.ds((so * 8 + s2 * 4) * toks, 4 * toks), :factor] = left[
                so * 4 * toks : (so + 1) * 4 * toks, s2 * factor : (s2 + 1) * factor
            ]
    eye = iota((seqs, seqs), 0) == iota((seqs, seqs), 1)
    mask = pack_ref[half].astype(F32)[:, :seqs]
    for i in range(toks):
        picked = jnp.where(eye, jnp.broadcast_to(mask[i : i + 1], (seqs, seqs)), 0.0)
        rows_i = left_scr[pl.ds(i, seqs, stride=toks), :][:, :factor].T.astype(BF16)
        rhs_scr[i // 2, :, i % 2 * 2 * seqs : (i % 2 + 1) * 2 * seqs] = twice(
            dot(rows_i, picked.astype(BF16))
        ).astype(BF16)
    copies[0].wait()
    weight_scr[...] = outer_ref[...].astype(F32)
    channels = outer_ref.shape[1]
    for ep in range(factor // 2):
        even = weight_scr[pl.ds(2 * ep, factor, stride=factor), :]
        odd = weight_scr[pl.ds(2 * ep + 1, factor, stride=factor), :]
        lhs_scr[ep * channels : (ep + 1) * channels, :] = jnp.concatenate(
            [even, odd], axis=0
        ).T.astype(BF16)

    def step(ip, carry):
        product = dot(lhs_scr[...], rhs_scr[ip]).astype(BF16)
        for ep in range(factor // 2):
            for i2 in range(2):
                folded_ref[2 * ip + i2, :, ep * 2 * seqs : (ep + 1) * 2 * seqs] = product[
                    ep * channels : (ep + 1) * channels, i2 * 2 * seqs : (i2 + 1) * 2 * seqs
                ]
        return carry

    lax.fori_loop(0, toks // 2, step, 0)
    copies[1].wait()


def gate_kernel(
    seqs,
    heads,
    pack_ref,
    latter_hbm,
    content_hbm,
    switch_hbm,
    final_hbm,
    gate_ref,
    right_ref,
    value_ref,
    result_ref,
    latter_ref,
    content_ref,
    switch_ref,
    final_ref,
    sems,
):
    copies = fetch(
        (latter_hbm, content_hbm, switch_hbm, final_hbm),
        (latter_ref, content_ref, switch_ref, final_ref),
        sems,
    )
    half, toks, lanes = seqs // 2, pack_ref.shape[1], pack_ref.shape[2]
    factor, width = latter_ref.shape
    rows = pack_ref[:half].reshape(half * toks, lanes)
    for copy in copies:
        copy.wait()
    spread = jnp.where(
        iota((8 * factor, factor), 0) // 8 == iota((8 * factor, factor), 1), 1.0, 0.0
    ).astype(BF16)
    tall = dot(spread, latter_ref[...])
    row = iota(tall.shape, 0) % 8
    right_ref[...] = jnp.concatenate(
        [jnp.where(row == s2 * 4 + rest, tall, 0.0) for rest in range(4) for s2 in range(2)], axis=1
    ).astype(BF16)
    column = content_ref.shape[1] // heads
    for hp in range(heads // 2):
        cols = slice(2 * column * hp, 2 * column * (hp + 1))
        gate_ref[hp] = jax.nn.sigmoid(dot(rows, twice(switch_ref[:, cols])))
        piece = content_ref[:, cols].astype(F32)
        which = iota(piece.shape, 1) // column
        zero = jnp.zeros_like(piece)
        for h2 in range(2):
            mine = jnp.where(which == h2, piece, 0.0)
            for s2 in range(2):
                base = (h2 * 2 + s2) * width
                row = [mine, zero] if s2 == 0 else [zero, mine]
                value_ref[hp, base : base + width, :] = jnp.concatenate(row, 1).astype(BF16)
        result_ref[hp] = twice(final_ref[:, cols])


def main_kernel(seqs, heads, shifts, *refs):
    blocks = refs[: len(shifts)]
    (
        rows_hbm,
        weight_hbm,
        gain_hbm,
        turned_ref,
        folded_ref,
        gate_ref,
        right_ref,
        value_ref,
        result_ref,
        out_ref,
        pair_hbm,
        rows_ref,
        weight_ref,
        gain_ref,
        pair_ref,
        mask_scr,
        rhs_scr,
        logits_scr,
        mixed_scr,
        even_scr,
        odd_scr,
        sems,
        pair_sem,
    ) = refs[len(shifts) :]
    copies = fetch(
        (weight_hbm, gain_hbm, rows_hbm),
        (weight_ref, gain_ref, rows_ref),
        sems,
    )
    half = seqs // 2
    outer = seqs // 8
    devs = len(shifts)
    _, toks, lanes = blocks[0].shape
    tokens = devs * toks
    tiles = tokens // 128
    spots = positions(devs, toks, shifts)

    def gathered(n):
        return jnp.concatenate([block[n] for block in blocks], axis=0)

    mask = gathered(half)
    own = jnp.where(iota((toks, lanes), 1) < seqs, blocks[0][half], 0)
    inverse = 1.0 / (1.0 + dot_nt(own, mask))
    pick = jnp.where(iota((seqs + 8, lanes), 0) == iota((seqs + 8, lanes), 1), 1.0, 0.0)
    mask_scr[...] = dot_nt(pick.astype(BF16), mask)
    real = mask_scr[seqs : seqs + 1, :]
    factor = rhs_scr.shape[0]
    for so in range(0, outer, 2):
        pieces = []
        for n in (so, so + 1):
            rows = jnp.concatenate([gathered(n * 4 + r) for r in range(4)], axis=1)
            right = dot_nt(right_ref[...], rows).reshape(factor, 8, tokens)
            pieces.append(right * mask_scr[n * 8 : n * 8 + 8, :])
        rhs_scr[:, so * 8 : so * 8 + 16, :] = jnp.concatenate(pieces, axis=1).astype(BF16)
    for copy in copies[:2]:
        copy.wait()
    w_high, w_low = split(weight_ref[...] * gain_ref[...])
    weights = jnp.concatenate([w_high, w_low], axis=0)
    w_sum = jnp.sum(w_high.astype(F32) + w_low.astype(F32), axis=1, keepdims=True)
    channels = turned_ref.shape[1]
    group = even_scr.shape[0] // channels

    def product(g, acc_scr):
        rows = folded_ref[g * group : (g + 1) * group].reshape(group * channels, -1)
        acc_scr[...] = dot(rows, rhs_scr[...].reshape(factor * seqs, tokens))

    def finish(g, acc_scr):
        for n in range(group):
            i = g * group + n
            for jb in range(tiles):
                cols = slice(jb * 128, (jb + 1) * 128)
                update = acc_scr[n * channels : (n + 1) * channels, cols] * inverse[i : i + 1, cols]
                x = (turned_ref[i, :, cols].astype(F32) + update).astype(BF16)
                logits = dot(weights, x)
                x = x.astype(F32)
                turned = x.T.astype(BF16)
                for k in range(128 // toks):
                    spot = spots[jb * (128 // toks) + k]
                    pair_ref[i, pl.ds(spot, toks), :] = turned[k * toks : (k + 1) * toks]
                mean = jnp.mean(x, axis=0, keepdims=True)
                x = x - mean
                scale = lax.rsqrt(jnp.mean(x * x, axis=0, keepdims=True) + 1e-05)
                logits = (logits[:heads] + logits[heads:] - w_sum * mean) * scale
                logits_scr[jb, pl.ds(i, heads, stride=toks), :] = logits
            pltpu.make_async_copy(pair_ref.at[i], pair_hbm.at[i], pair_sem.at[i]).start()

    scratch = (even_scr, odd_scr)
    product(0, even_scr)
    for g in range(toks // group):
        if g + 1 < toks // group:
            product(g + 1, scratch[(g + 1) % 2])
        finish(g, scratch[g % 2])
    logits = jnp.concatenate([logits_scr[jb] for jb in range(tiles)], axis=1)
    logits = jnp.where(real > 0.5, logits, -1000000000.0)
    top = jnp.max(logits, axis=-1, keepdims=True)
    power = jnp.exp(logits - top)
    probs = (power / jnp.sum(power, axis=-1, keepdims=True)).astype(BF16)
    for b in range(0, half, 2):
        mixed = dot(probs, jnp.concatenate([gathered(b), gathered(b + 1)], axis=1)).astype(BF16)
        mixed_scr[b] = mixed[:, :lanes]
        mixed_scr[b + 1] = mixed[:, lanes:]
    total = None
    for hp in range(heads // 2):
        pair = jnp.concatenate(
            [
                mixed_scr[:, (2 * hp + h2) * toks : (2 * hp + h2 + 1) * toks, :].reshape(
                    half * toks, lanes
                )
                for h2 in range(2)
            ],
            axis=1,
        )
        average = dot(pair, value_ref[hp])
        gated = (gate_ref[hp] * average).astype(BF16)
        part = dot_nt(gated, result_ref[hp])
        total = part if total is None else total + part
    copies[2].wait()
    width = rows_ref.shape[2]
    total = total.reshape(outer, 4, toks, lanes)
    base = rows_ref[...].astype(F32).reshape(outer, 2, 4, toks, width)
    for s2 in range(2):
        piece = base[:, s2] + total[..., s2 * width : (s2 + 1) * width]
        for so in range(outer):
            out_ref[so * 8 + s2 * 4 : so * 8 + s2 * 4 + 4] = piece[so].astype(BF16)
    for i in range(toks):
        pltpu.make_async_copy(pair_ref.at[i], pair_hbm.at[i], pair_sem.at[i]).wait()


def far_order(devs):
    far = list(range(4, devs, 4))
    return far[:1] + far[:0:-1]


def shards(
    homolog_embedding,
    pair_state_tiles,
    alignment_mask,
    token_real_mask,
    lineup_standardize_scaling,
    former_factor_proj,
    latter_factor_proj,
    outer_output_weight,
    pair_norm_gain,
    pair_logit_weight,
    content_vector_proj,
    sigmoid_switch_proj,
    final_result_proj,
    *,
    devs,
):
    seqs, toks, width = homolog_embedding.shape
    tokens = devs * toks
    heads = pair_logit_weight.shape[1]
    factor = former_factor_proj.shape[1]
    channels = outer_output_weight.shape[1]
    lanes = 2 * width
    half = seqs // 2
    params = pltpu.CompilerParams(vmem_limit_bytes=28 << 20)

    def keep(*arrays):
        return [pltpu.with_memory_space_constraint(a, pltpu.HBM) for a in arrays]

    def room(*arrays):
        return [pltpu.VMEM(a.shape, a.dtype) for a in arrays]

    arrays = (
        homolog_embedding,
        alignment_mask.T,
        lineup_standardize_scaling[None],
        token_real_mask[None],
    )
    packed, former = pl.pallas_call(
        pack_kernel,
        out_shape=(
            jax.ShapeDtypeStruct((half + 1, toks, lanes), BF16),
            jax.ShapeDtypeStruct((factor, width), BF16),
        ),
        in_specs=[HB] * 5,
        out_specs=(VM,) * 2,
        scratch_shapes=room(*arrays) + [pltpu.SemaphoreType.DMA((5,))],
        compiler_params=params,
        name="pack",
    )(*keep(*arrays, former_factor_proj.T))

    def swap(block, shift):
        return lax.ppermute(block, "row", [(n, n ^ shift) for n in range(devs)])

    held = {0: packed}
    far = far_order(devs)
    for shift in far:
        held[shift] = swap(packed, shift)
    for bit in (2, 1):
        for shift in list(held):
            held[shift ^ bit] = swap(held[shift], bit)
    shifts = tuple(sorted(held))

    folded, state = pl.pallas_call(
        functools.partial(fold_kernel, seqs),
        out_shape=(
            jax.ShapeDtypeStruct((toks, channels, factor * seqs), BF16),
            jax.ShapeDtypeStruct(pair_state_tiles.shape, BF16),
        ),
        in_specs=[VM] * 2 + [HB] * 2,
        out_specs=(VM,) * 2,
        scratch_shapes=room(outer_output_weight)
        + [
            pltpu.VMEM(outer_output_weight.shape, F32),
            pltpu.VMEM((seqs * toks, 128), F32),
            pltpu.VMEM((factor // 2 * channels, 2 * factor), BF16),
            pltpu.VMEM((toks // 2, 2 * factor, 4 * seqs), BF16),
            pltpu.SemaphoreType.DMA((2,)),
        ],
        compiler_params=params,
        cost_estimate=pl.CostEstimate(flops=10**9, bytes_accessed=10**7, transcendentals=0),
        name="fold",
    )(packed, former, *keep(outer_output_weight, pair_state_tiles))
    arrays = (
        latter_factor_proj.T,
        content_vector_proj,
        sigmoid_switch_proj,
        final_result_proj.T,
    )
    gate, right, value, result = pl.pallas_call(
        functools.partial(gate_kernel, seqs, heads),
        out_shape=(
            jax.ShapeDtypeStruct((heads // 2, half * toks, lanes), F32),
            jax.ShapeDtypeStruct((8 * factor, 8 * width), BF16),
            jax.ShapeDtypeStruct((heads // 2, 4 * width, lanes), BF16),
            jax.ShapeDtypeStruct((heads // 2, lanes, lanes), BF16),
        ),
        in_specs=[VM] + [HB] * 4,
        out_specs=(VM,) * 4,
        scratch_shapes=room(*arrays) + [pltpu.SemaphoreType.DMA((4,))],
        compiler_params=params,
        cost_estimate=pl.CostEstimate(
            flops=10**8, bytes_accessed=10**6, transcendentals=10**6
        ),
        name="gate",
    )(packed, *keep(*arrays))
    turned = pl.pallas_call(
        functools.partial(turn_kernel, shifts),
        out_shape=jax.ShapeDtypeStruct((toks, channels, tokens), BF16),
        in_specs=[VM],
        out_specs=VM,
        compiler_params=params,
        cost_estimate=pl.CostEstimate(flops=10**7, bytes_accessed=10**6, transcendentals=0),
        name="turn",
    )(state)
    arrays = (homolog_embedding, pair_logit_weight.T, pair_norm_gain[None])
    group = GROUP
    out, pair = pl.pallas_call(
        functools.partial(main_kernel, seqs, heads, shifts),
        out_shape=(
            jax.ShapeDtypeStruct(homolog_embedding.shape, BF16),
            jax.ShapeDtypeStruct(pair_state_tiles.shape, BF16),
        ),
        in_specs=[VM] * devs + [HB] * 3 + [VM] * 6,
        out_specs=(VM, HB),
        scratch_shapes=room(*arrays)
        + [
            pltpu.VMEM(pair_state_tiles.shape, BF16),
            pltpu.VMEM((seqs + 8, tokens), F32),
            pltpu.VMEM((factor, seqs, tokens), BF16),
            pltpu.VMEM((tokens // 128, heads * toks, 128), F32),
            pltpu.VMEM((half, heads * toks, lanes), BF16),
            pltpu.VMEM((group * channels, tokens), F32),
            pltpu.VMEM((group * channels, tokens), F32),
            pltpu.SemaphoreType.DMA((3,)),
            pltpu.SemaphoreType.DMA((toks,)),
        ],
        compiler_params=params,
        cost_estimate=pl.CostEstimate(flops=4 * 10**9, bytes_accessed=10**7, transcendentals=10**6),
        name="main",
    )(
        *[held[shift] for shift in shifts],
        *keep(*arrays),
        turned,
        folded,
        gate,
        right,
        value,
        result,
    )
    return out, pair


def solution(mesh):
    placed = (
        P("groups", "row", None),
        P(("groups", "row"), None, None),
        P("groups", "row"),
        P("groups"),
        P(),
        P(),
        P(),
        P(),
        P(),
        P(),
        P(),
        P(),
        P(),
    )
    devs = mesh.shape["row"]

    def body(*arrays):
        return shards(*arrays, devs=devs)

    return jax.shard_map(
        body,
        mesh=mesh,
        in_specs=placed,
        out_specs=(P("groups", "row", None), P(("groups", "row"), None, None)),
        check_vma=False,
    )
```

```python
import functools

import jax
import jax.numpy as jnp
from jax import lax
from jax.experimental import pallas as pl
from jax.experimental.pallas import tpu as pltpu
from jax.sharding import PartitionSpec as P


F32 = jnp.float32
BF16 = jnp.bfloat16
VM = pl.BlockSpec(memory_space=pltpu.VMEM)
GROUP = 4
HB = pl.BlockSpec(memory_space=pltpu.HBM)


def dot(a, b):
    return jnp.dot(a, b, preferred_element_type=F32)


def dot_nt(a, b):
    return lax.dot_general(a, b, (((1,), (1,)), ((), ())), preferred_element_type=F32)


def iota(shape, axis):
    return lax.broadcasted_iota(jnp.int32, shape, axis)


def split(x):
    high = x.astype(BF16)
    return high, (x - high.astype(F32)).astype(BF16)


def twice(block):
    zero = jnp.zeros_like(block)
    return jnp.concatenate(
        [jnp.concatenate([block, zero], 1), jnp.concatenate([zero, block], 1)], 0
    )


def fetch(sources, targets, sems):
    copies = [pltpu.make_async_copy(a, b, sems.at[n]) for n, (a, b) in enumerate(zip(sources, targets))]
    for copy in copies:
        copy.start()
    return copies


def pack_kernel(
    rows_hbm,
    mask_hbm,
    gain_hbm,
    real_hbm,
    former_hbm,
    out_ref,
    former_ref,
    rows_ref,
    mask_ref,
    gain_ref,
    real_ref,
    sems,
):
    copies = fetch(
        (rows_hbm, mask_hbm, gain_hbm, real_hbm, former_hbm),
        (rows_ref, mask_ref, gain_ref, real_ref, former_ref),
        sems,
    )
    for copy in copies:
        copy.wait()
    seqs, toks, width = rows_ref.shape
    outer = seqs // 8
    x = rows_ref[...].reshape(outer, 2, 4, toks, width)
    x = jnp.concatenate([x[:, 0], x[:, 1]], axis=-1).reshape(seqs // 2 * toks, 2 * width)
    lanes = 2 * width
    same = (iota((lanes, lanes), 0) // width) == (iota((lanes, lanes), 1) // width)
    mean_of = jnp.where(same, 1.0 / width, 0.0).astype(BF16)
    centered = x.astype(F32) - dot(x, mean_of)
    high, low = split(centered * centered)
    spread = dot(high, mean_of) + dot(low, mean_of)
    gain = jnp.concatenate([gain_ref[...], gain_ref[...]], axis=-1)
    normed = centered * lax.rsqrt(spread + 1e-05) * gain
    out_ref[: seqs // 2] = normed.astype(BF16).reshape(seqs // 2, toks, lanes)
    real = real_ref[...].astype(F32)
    tokens = real.shape[1]
    here = iota((toks, tokens), 1) == lax.axis_index("row") * toks + iota((toks, tokens), 0)
    mine = jnp.sum(jnp.where(here, real, 0.0), axis=1, keepdims=True)
    mask = mask_ref[...].astype(F32)
    mask = jnp.concatenate([mask, jnp.zeros((toks, lanes - seqs), F32)], axis=-1)
    mask = jnp.where(iota(mask.shape, 1) == seqs, mine, mask)
    out_ref[seqs // 2] = mask.astype(BF16)


def positions(devs, toks, shifts):
    me = lax.axis_index("row")
    spots = []
    for shift in shifts:
        where = 0
        bit = 1
        while bit < devs:
            mine = (me // bit) % 2
            where = where + bit * ((1 - mine) if shift & bit else mine)
            bit *= 2
        spots.append(pl.multiple_of(where * toks, toks))
    return spots


def turn_kernel(shifts, state_ref, turned_ref):
    toks = state_ref.shape[0]
    spots = positions(len(shifts), toks, shifts)
    group = 128 // toks
    for i in range(toks):
        for jb in range(len(shifts) // group):
            rows = [
                state_ref[i, pl.ds(spot, toks), :] for spot in spots[jb * group : (jb + 1) * group]
            ]
            block = jnp.concatenate(rows, axis=0).astype(F32).T
            turned_ref[i, :, jb * 128 : (jb + 1) * 128] = block.astype(BF16)


def fold_kernel(
    seqs,
    pack_ref,
    former_ref,
    outer_hbm,
    state_hbm,
    folded_ref,
    state_ref,
    outer_ref,
    weight_scr,
    left_scr,
    lhs_scr,
    rhs_scr,
    sems,
):
    copies = fetch((outer_hbm, state_hbm), (outer_ref, state_ref), sems)
    half, toks, lanes = seqs // 2, pack_ref.shape[1], pack_ref.shape[2]
    factor, _ = former_ref.shape
    outer = seqs // 8
    rows = pack_ref[:half].reshape(half * toks, lanes)
    left = dot_nt(rows, twice(former_ref[...]))
    for so in range(outer):
        for s2 in range(2):
            left_scr[pl.ds((so * 8 + s2 * 4) * toks, 4 * toks), :factor] = left[
                so * 4 * toks : (so + 1) * 4 * toks, s2 * factor : (s2 + 1) * factor
            ]
    eye = iota((seqs, seqs), 0) == iota((seqs, seqs), 1)
    mask = pack_ref[half].astype(F32)[:, :seqs]
    for i in range(toks):
        picked = jnp.where(eye, jnp.broadcast_to(mask[i : i + 1], (seqs, seqs)), 0.0)
        rows_i = left_scr[pl.ds(i, seqs, stride=toks), :][:, :factor].T.astype(BF16)
        rhs_scr[i // 2, :, i % 2 * 2 * seqs : (i % 2 + 1) * 2 * seqs] = twice(
            dot(rows_i, picked.astype(BF16))
        ).astype(BF16)
    copies[0].wait()
    weight_scr[...] = outer_ref[...].astype(F32)
    channels = outer_ref.shape[1]
    for ep in range(factor // 2):
        even = weight_scr[pl.ds(2 * ep, factor, stride=factor), :]
        odd = weight_scr[pl.ds(2 * ep + 1, factor, stride=factor), :]
        lhs_scr[ep * channels : (ep + 1) * channels, :] = jnp.concatenate(
            [even, odd], axis=0
        ).T.astype(BF16)

    def step(ip, carry):
        product = dot(lhs_scr[...], rhs_scr[ip]).astype(BF16)
        for ep in range(factor // 2):
            for i2 in range(2):
                folded_ref[2 * ip + i2, :, ep * 2 * seqs : (ep + 1) * 2 * seqs] = product[
                    ep * channels : (ep + 1) * channels, i2 * 2 * seqs : (i2 + 1) * 2 * seqs
                ]
        return carry

    lax.fori_loop(0, toks // 2, step, 0)
    copies[1].wait()


def gate_kernel(
    seqs,
    heads,
    pack_ref,
    latter_hbm,
    content_hbm,
    switch_hbm,
    final_hbm,
    gate_ref,
    right_ref,
    value_ref,
    result_ref,
    latter_ref,
    content_ref,
    switch_ref,
    final_ref,
    sems,
):
    copies = fetch(
        (latter_hbm, content_hbm, switch_hbm, final_hbm),
        (latter_ref, content_ref, switch_ref, final_ref),
        sems,
    )
    half, toks, lanes = seqs // 2, pack_ref.shape[1], pack_ref.shape[2]
    factor, width = latter_ref.shape
    rows = pack_ref[:half].reshape(half * toks, lanes)
    for copy in copies:
        copy.wait()
    spread = jnp.where(
        iota((8 * factor, factor), 0) // 8 == iota((8 * factor, factor), 1), 1.0, 0.0
    ).astype(BF16)
    tall = dot(spread, latter_ref[...])
    row = iota(tall.shape, 0) % 8
    right_ref[...] = jnp.concatenate(
        [jnp.where(row == s2 * 4 + rest, tall, 0.0) for rest in range(4) for s2 in range(2)], axis=1
    ).astype(BF16)
    column = content_ref.shape[1] // heads
    for hp in range(heads // 2):
        cols = slice(2 * column * hp, 2 * column * (hp + 1))
        gate_ref[hp] = jax.nn.sigmoid(dot(rows, twice(switch_ref[:, cols])))
        piece = content_ref[:, cols].astype(F32)
        which = iota(piece.shape, 1) // column
        zero = jnp.zeros_like(piece)
        for h2 in range(2):
            mine = jnp.where(which == h2, piece, 0.0)
            for s2 in range(2):
                base = (h2 * 2 + s2) * width
                row = [mine, zero] if s2 == 0 else [zero, mine]
                value_ref[hp, base : base + width, :] = jnp.concatenate(row, 1).astype(BF16)
        result_ref[hp] = twice(final_ref[:, cols])


def main_kernel(seqs, heads, shifts, *refs):
    blocks = refs[: len(shifts)]
    (
        rows_hbm,
        weight_hbm,
        gain_hbm,
        turned_ref,
        folded_ref,
        gate_ref,
        right_ref,
        value_ref,
        result_ref,
        out_hbm,
        pair_hbm,
        rows_ref,
        weight_ref,
        gain_ref,
        out_ref,
        pair_ref,
        mask_scr,
        rhs_scr,
        logits_scr,
        mixed_scr,
        even_scr,
        odd_scr,
        sems,
        pair_sem,
    ) = refs[len(shifts) :]
    copies = fetch(
        (weight_hbm, gain_hbm, rows_hbm),
        (weight_ref, gain_ref, rows_ref),
        sems,
    )
    half = seqs // 2
    outer = seqs // 8
    devs = len(shifts)
    _, toks, lanes = blocks[0].shape
    tokens = devs * toks
    tiles = tokens // 128
    spots = positions(devs, toks, shifts)

    def gathered(n):
        return jnp.concatenate([block[n] for block in blocks], axis=0)

    mask = gathered(half)
    own = jnp.where(iota((toks, lanes), 1) < seqs, blocks[0][half], 0)
    inverse = 1.0 / (1.0 + dot_nt(own, mask))
    pick = jnp.where(iota((seqs + 8, lanes), 0) == iota((seqs + 8, lanes), 1), 1.0, 0.0)
    mask_scr[...] = dot_nt(pick.astype(BF16), mask)
    real = mask_scr[seqs : seqs + 1, :]
    factor = rhs_scr.shape[0]
    for so in range(0, outer, 2):
        pieces = []
        for n in (so, so + 1):
            rows = jnp.concatenate([gathered(n * 4 + r) for r in range(4)], axis=1)
            right = dot_nt(right_ref[...], rows).reshape(factor, 8, tokens)
            pieces.append(right * mask_scr[n * 8 : n * 8 + 8, :])
        rhs_scr[:, so * 8 : so * 8 + 16, :] = jnp.concatenate(pieces, axis=1).astype(BF16)
    for copy in copies[:2]:
        copy.wait()
    w_high, w_low = split(weight_ref[...] * gain_ref[...])
    weights = jnp.concatenate([w_high, w_low], axis=0)
    w_sum = jnp.sum(w_high.astype(F32) + w_low.astype(F32), axis=1, keepdims=True)
    channels = turned_ref.shape[1]
    group = even_scr.shape[0] // channels

    def product(g, acc_scr):
        rows = folded_ref[g * group : (g + 1) * group].reshape(group * channels, -1)
        acc_scr[...] = dot(rows, rhs_scr[...].reshape(factor * seqs, tokens))

    def finish(g, acc_scr):
        for n in range(group):
            i = g * group + n
            for jb in range(tiles):
                cols = slice(jb * 128, (jb + 1) * 128)
                update = acc_scr[n * channels : (n + 1) * channels, cols] * inverse[i : i + 1, cols]
                x = (turned_ref[i, :, cols].astype(F32) + update).astype(BF16)
                logits = dot(weights, x)
                x = x.astype(F32)
                turned = x.T.astype(BF16)
                for k in range(128 // toks):
                    spot = spots[jb * (128 // toks) + k]
                    pair_ref[i, pl.ds(spot, toks), :] = turned[k * toks : (k + 1) * toks]
                mean = jnp.mean(x, axis=0, keepdims=True)
                x = x - mean
                scale = lax.rsqrt(jnp.mean(x * x, axis=0, keepdims=True) + 1e-05)
                logits = (logits[:heads] + logits[heads:] - w_sum * mean) * scale
                logits_scr[jb, pl.ds(i, heads, stride=toks), :] = logits
            pltpu.make_async_copy(pair_ref.at[i], pair_hbm.at[i], pair_sem.at[i]).start()

    scratch = (even_scr, odd_scr)
    product(0, even_scr)
    for g in range(toks // group):
        if g + 1 < toks // group:
            product(g + 1, scratch[(g + 1) % 2])
        finish(g, scratch[g % 2])
    logits = jnp.concatenate([logits_scr[jb] for jb in range(tiles)], axis=1)
    logits = jnp.where(real > 0.5, logits, -1000000000.0)
    top = jnp.max(logits, axis=-1, keepdims=True)
    power = jnp.exp(logits - top)
    probs = (power / jnp.sum(power, axis=-1, keepdims=True)).astype(BF16)
    for b in range(0, half, 2):
        mixed = dot(probs, jnp.concatenate([gathered(b), gathered(b + 1)], axis=1)).astype(BF16)
        mixed_scr[b] = mixed[:, :lanes]
        mixed_scr[b + 1] = mixed[:, lanes:]
    total = None
    for hp in range(heads // 2):
        pair = jnp.concatenate(
            [
                mixed_scr[:, (2 * hp + h2) * toks : (2 * hp + h2 + 1) * toks, :].reshape(
                    half * toks, lanes
                )
                for h2 in range(2)
            ],
            axis=1,
        )
        average = dot(pair, value_ref[hp])
        gated = (gate_ref[hp] * average).astype(BF16)
        part = dot_nt(gated, result_ref[hp])
        total = part if total is None else total + part
    copies[2].wait()
    width = rows_ref.shape[2]
    total = total.reshape(outer, 4, toks, lanes)
    base = rows_ref[...].astype(F32).reshape(outer, 2, 4, toks, width)
    stores = []
    for so in range(outer):
        for s2 in range(2):
            piece = base[so, s2] + total[so, ..., s2 * width : (s2 + 1) * width]
            out_ref[so * 8 + s2 * 4 : so * 8 + s2 * 4 + 4] = piece.astype(BF16)
        if so % 2:
            here = pl.ds(so // 2 * 16, 16)
            stores.append(
                pltpu.make_async_copy(out_ref.at[here], out_hbm.at[here], sems.at[3 + so // 2])
            )
            stores[-1].start()
    for i in range(toks):
        pltpu.make_async_copy(pair_ref.at[i], pair_hbm.at[i], pair_sem.at[i]).wait()
    for store in stores:
        store.wait()


def far_order(devs):
    far = list(range(4, devs, 4))
    return far[:1] + far[:0:-1]


def shards(
    homolog_embedding,
    pair_state_tiles,
    alignment_mask,
    token_real_mask,
    lineup_standardize_scaling,
    former_factor_proj,
    latter_factor_proj,
    outer_output_weight,
    pair_norm_gain,
    pair_logit_weight,
    content_vector_proj,
    sigmoid_switch_proj,
    final_result_proj,
    *,
    devs,
):
    seqs, toks, width = homolog_embedding.shape
    tokens = devs * toks
    heads = pair_logit_weight.shape[1]
    factor = former_factor_proj.shape[1]
    channels = outer_output_weight.shape[1]
    lanes = 2 * width
    half, outer = seqs // 2, seqs // 8
    params = pltpu.CompilerParams(vmem_limit_bytes=28 << 20)

    def keep(*arrays):
        return [pltpu.with_memory_space_constraint(a, pltpu.HBM) for a in arrays]

    def room(*arrays):
        return [pltpu.VMEM(a.shape, a.dtype) for a in arrays]

    arrays = (
        homolog_embedding,
        alignment_mask.T,
        lineup_standardize_scaling[None],
        token_real_mask[None],
    )
    packed, former = pl.pallas_call(
        pack_kernel,
        out_shape=(
            jax.ShapeDtypeStruct((half + 1, toks, lanes), BF16),
            jax.ShapeDtypeStruct((factor, width), BF16),
        ),
        in_specs=[HB] * 5,
        out_specs=(VM,) * 2,
        scratch_shapes=room(*arrays) + [pltpu.SemaphoreType.DMA((5,))],
        compiler_params=params,
        name="pack",
    )(*keep(*arrays, former_factor_proj.T))

    def swap(block, shift):
        return lax.ppermute(block, "row", [(n, n ^ shift) for n in range(devs)])

    held = {0: packed}
    far = far_order(devs)
    for shift in far:
        held[shift] = swap(packed, shift)
    for bit in (2, 1):
        for shift in list(held):
            held[shift ^ bit] = swap(held[shift], bit)
    shifts = tuple(sorted(held))

    folded, state = pl.pallas_call(
        functools.partial(fold_kernel, seqs),
        out_shape=(
            jax.ShapeDtypeStruct((toks, channels, factor * seqs), BF16),
            jax.ShapeDtypeStruct(pair_state_tiles.shape, BF16),
        ),
        in_specs=[VM] * 2 + [HB] * 2,
        out_specs=(VM,) * 2,
        scratch_shapes=room(outer_output_weight)
        + [
            pltpu.VMEM(outer_output_weight.shape, F32),
            pltpu.VMEM((seqs * toks, 128), F32),
            pltpu.VMEM((factor // 2 * channels, 2 * factor), BF16),
            pltpu.VMEM((toks // 2, 2 * factor, 4 * seqs), BF16),
            pltpu.SemaphoreType.DMA((2,)),
        ],
        compiler_params=params,
        cost_estimate=pl.CostEstimate(flops=10**9, bytes_accessed=10**7, transcendentals=0),
        name="fold",
    )(packed, former, *keep(outer_output_weight, pair_state_tiles))
    arrays = (
        latter_factor_proj.T,
        content_vector_proj,
        sigmoid_switch_proj,
        final_result_proj.T,
    )
    gate, right, value, result = pl.pallas_call(
        functools.partial(gate_kernel, seqs, heads),
        out_shape=(
            jax.ShapeDtypeStruct((heads // 2, half * toks, lanes), F32),
            jax.ShapeDtypeStruct((8 * factor, 8 * width), BF16),
            jax.ShapeDtypeStruct((heads // 2, 4 * width, lanes), BF16),
            jax.ShapeDtypeStruct((heads // 2, lanes, lanes), BF16),
        ),
        in_specs=[VM] + [HB] * 4,
        out_specs=(VM,) * 4,
        scratch_shapes=room(*arrays) + [pltpu.SemaphoreType.DMA((4,))],
        compiler_params=params,
        cost_estimate=pl.CostEstimate(
            flops=10**8, bytes_accessed=10**6, transcendentals=10**6
        ),
        name="gate",
    )(packed, *keep(*arrays))
    turned = pl.pallas_call(
        functools.partial(turn_kernel, shifts),
        out_shape=jax.ShapeDtypeStruct((toks, channels, tokens), BF16),
        in_specs=[VM],
        out_specs=VM,
        compiler_params=params,
        cost_estimate=pl.CostEstimate(flops=10**7, bytes_accessed=10**6, transcendentals=0),
        name="turn",
    )(state)
    arrays = (homolog_embedding, pair_logit_weight.T, pair_norm_gain[None])
    group = GROUP
    out, pair = pl.pallas_call(
        functools.partial(main_kernel, seqs, heads, shifts),
        out_shape=(
            jax.ShapeDtypeStruct(homolog_embedding.shape, BF16),
            jax.ShapeDtypeStruct(pair_state_tiles.shape, BF16),
        ),
        in_specs=[VM] * devs + [HB] * 3 + [VM] * 6,
        out_specs=(HB, HB),
        scratch_shapes=room(*arrays, homolog_embedding)
        + [
            pltpu.VMEM(pair_state_tiles.shape, BF16),
            pltpu.VMEM((seqs + 8, tokens), F32),
            pltpu.VMEM((factor, seqs, tokens), BF16),
            pltpu.VMEM((tokens // 128, heads * toks, 128), F32),
            pltpu.VMEM((half, heads * toks, lanes), BF16),
            pltpu.VMEM((group * channels, tokens), F32),
            pltpu.VMEM((group * channels, tokens), F32),
            pltpu.SemaphoreType.DMA((3 + outer // 2,)),
            pltpu.SemaphoreType.DMA((toks,)),
        ],
        compiler_params=params,
        cost_estimate=pl.CostEstimate(flops=4 * 10**9, bytes_accessed=10**7, transcendentals=10**6),
        name="main",
    )(
        *[held[shift] for shift in shifts],
        *keep(*arrays),
        turned,
        folded,
        gate,
        right,
        value,
        result,
    )
    return out, pair


def solution(mesh):
    placed = (
        P("groups", "row", None),
        P(("groups", "row"), None, None),
        P("groups", "row"),
        P("groups"),
        P(),
        P(),
        P(),
        P(),
        P(),
        P(),
        P(),
        P(),
        P(),
    )
    devs = mesh.shape["row"]

    def body(*arrays):
        return shards(*arrays, devs=devs)

    return jax.shard_map(
        body,
        mesh=mesh,
        in_specs=placed,
        out_specs=(P("groups", "row", None), P(("groups", "row"), None, None)),
        check_vma=False,
    )
```

```python
import functools

import jax
import jax.numpy as jnp
from jax import lax
from jax.experimental import pallas as pl
from jax.experimental.pallas import tpu as pltpu
from jax.sharding import PartitionSpec as P


F32 = jnp.float32
BF16 = jnp.bfloat16
VM = pl.BlockSpec(memory_space=pltpu.VMEM)
GROUP = 4
HB = pl.BlockSpec(memory_space=pltpu.HBM)


def dot(a, b):
    return jnp.dot(a, b, preferred_element_type=F32)


def dot_nt(a, b):
    return lax.dot_general(a, b, (((1,), (1,)), ((), ())), preferred_element_type=F32)


def iota(shape, axis):
    return lax.broadcasted_iota(jnp.int32, shape, axis)


def split(x):
    high = x.astype(BF16)
    return high, (x - high.astype(F32)).astype(BF16)


def twice(block):
    zero = jnp.zeros_like(block)
    return jnp.concatenate(
        [jnp.concatenate([block, zero], 1), jnp.concatenate([zero, block], 1)], 0
    )


def fetch(sources, targets, sems):
    copies = [pltpu.make_async_copy(a, b, sems.at[n]) for n, (a, b) in enumerate(zip(sources, targets))]
    for copy in copies:
        copy.start()
    return copies


def pack_kernel(
    rows_hbm,
    mask_hbm,
    gain_hbm,
    real_hbm,
    former_hbm,
    out_ref,
    former_ref,
    rows_ref,
    mask_ref,
    gain_ref,
    real_ref,
    sems,
):
    copies = fetch(
        (rows_hbm, mask_hbm, gain_hbm, real_hbm, former_hbm),
        (rows_ref, mask_ref, gain_ref, real_ref, former_ref),
        sems,
    )
    for copy in copies:
        copy.wait()
    seqs, toks, width = rows_ref.shape
    outer = seqs // 8
    x = rows_ref[...].reshape(outer, 2, 4, toks, width)
    x = jnp.concatenate([x[:, 0], x[:, 1]], axis=-1).reshape(seqs // 2 * toks, 2 * width)
    lanes = 2 * width
    same = (iota((lanes, lanes), 0) // width) == (iota((lanes, lanes), 1) // width)
    mean_of = jnp.where(same, 1.0 / width, 0.0).astype(BF16)
    centered = x.astype(F32) - dot(x, mean_of)
    high, low = split(centered * centered)
    spread = dot(high, mean_of) + dot(low, mean_of)
    gain = jnp.concatenate([gain_ref[...], gain_ref[...]], axis=-1)
    normed = centered * lax.rsqrt(spread + 1e-05) * gain
    out_ref[: seqs // 2] = normed.astype(BF16).reshape(seqs // 2, toks, lanes)
    real = real_ref[...].astype(F32)
    tokens = real.shape[1]
    here = iota((toks, tokens), 1) == lax.axis_index("row") * toks + iota((toks, tokens), 0)
    mine = jnp.sum(jnp.where(here, real, 0.0), axis=1, keepdims=True)
    mask = mask_ref[...].astype(F32)
    mask = jnp.concatenate([mask, jnp.zeros((toks, lanes - seqs), F32)], axis=-1)
    mask = jnp.where(iota(mask.shape, 1) == seqs, mine, mask)
    out_ref[seqs // 2] = mask.astype(BF16)


def positions(devs, toks, shifts):
    me = lax.axis_index("row")
    spots = []
    for shift in shifts:
        where = 0
        bit = 1
        while bit < devs:
            mine = (me // bit) % 2
            where = where + bit * ((1 - mine) if shift & bit else mine)
            bit *= 2
        spots.append(pl.multiple_of(where * toks, toks))
    return spots


def turn_kernel(shifts, state_ref, turned_ref):
    toks = state_ref.shape[0]
    spots = positions(len(shifts), toks, shifts)
    group = 128 // toks
    for i in range(toks):
        for jb in range(len(shifts) // group):
            rows = [
                state_ref[i, pl.ds(spot, toks), :] for spot in spots[jb * group : (jb + 1) * group]
            ]
            block = jnp.concatenate(rows, axis=0).astype(F32).T
            turned_ref[i, :, jb * 128 : (jb + 1) * 128] = block.astype(BF16)


def fold_kernel(
    seqs,
    pack_ref,
    former_ref,
    outer_hbm,
    state_hbm,
    folded_ref,
    state_ref,
    outer_ref,
    weight_scr,
    left_scr,
    lhs_scr,
    rhs_scr,
    sems,
):
    copies = fetch((outer_hbm, state_hbm), (outer_ref, state_ref), sems)
    half, toks, lanes = seqs // 2, pack_ref.shape[1], pack_ref.shape[2]
    factor, _ = former_ref.shape
    outer = seqs // 8
    rows = pack_ref[:half].reshape(half * toks, lanes)
    left = dot_nt(rows, twice(former_ref[...]))
    for so in range(outer):
        for s2 in range(2):
            left_scr[pl.ds((so * 8 + s2 * 4) * toks, 4 * toks), :factor] = left[
                so * 4 * toks : (so + 1) * 4 * toks, s2 * factor : (s2 + 1) * factor
            ]
    eye = iota((seqs, seqs), 0) == iota((seqs, seqs), 1)
    mask = pack_ref[half].astype(F32)[:, :seqs]
    for i in range(toks):
        picked = jnp.where(eye, jnp.broadcast_to(mask[i : i + 1], (seqs, seqs)), 0.0)
        rows_i = left_scr[pl.ds(i, seqs, stride=toks), :][:, :factor].T.astype(BF16)
        rhs_scr[i // 2, :, i % 2 * 2 * seqs : (i % 2 + 1) * 2 * seqs] = twice(
            dot(rows_i, picked.astype(BF16))
        ).astype(BF16)
    copies[0].wait()
    weight_scr[...] = outer_ref[...].astype(F32)
    channels = outer_ref.shape[1]
    for ep in range(factor // 2):
        even = weight_scr[pl.ds(2 * ep, factor, stride=factor), :]
        odd = weight_scr[pl.ds(2 * ep + 1, factor, stride=factor), :]
        lhs_scr[ep * channels : (ep + 1) * channels, :] = jnp.concatenate(
            [even, odd], axis=0
        ).T.astype(BF16)

    def step(ip, carry):
        product = dot(lhs_scr[...], rhs_scr[ip]).astype(BF16)
        for ep in range(factor // 2):
            for i2 in range(2):
                folded_ref[2 * ip + i2, :, ep * 2 * seqs : (ep + 1) * 2 * seqs] = product[
                    ep * channels : (ep + 1) * channels, i2 * 2 * seqs : (i2 + 1) * 2 * seqs
                ]
        return carry

    lax.fori_loop(0, toks // 2, step, 0)
    copies[1].wait()


def gate_kernel(
    seqs,
    heads,
    pack_ref,
    latter_hbm,
    content_hbm,
    switch_hbm,
    final_hbm,
    weight_hbm,
    gain_hbm,
    rows_hbm,
    gate_ref,
    right_ref,
    value_ref,
    result_ref,
    weight_ref,
    gain_ref,
    rows_ref,
    latter_ref,
    content_ref,
    switch_ref,
    final_ref,
    sems,
):
    copies = fetch(
        (latter_hbm, content_hbm, switch_hbm, final_hbm, weight_hbm, gain_hbm, rows_hbm),
        (latter_ref, content_ref, switch_ref, final_ref, weight_ref, gain_ref, rows_ref),
        sems,
    )
    half, toks, lanes = seqs // 2, pack_ref.shape[1], pack_ref.shape[2]
    factor, width = latter_ref.shape
    rows = pack_ref[:half].reshape(half * toks, lanes)
    for copy in copies[:4]:
        copy.wait()
    spread = jnp.where(
        iota((8 * factor, factor), 0) // 8 == iota((8 * factor, factor), 1), 1.0, 0.0
    ).astype(BF16)
    tall = dot(spread, latter_ref[...])
    row = iota(tall.shape, 0) % 8
    right_ref[...] = jnp.concatenate(
        [jnp.where(row == s2 * 4 + rest, tall, 0.0) for rest in range(4) for s2 in range(2)], axis=1
    ).astype(BF16)
    column = content_ref.shape[1] // heads
    for hp in range(heads // 2):
        cols = slice(2 * column * hp, 2 * column * (hp + 1))
        gate_ref[hp] = jax.nn.sigmoid(dot(rows, twice(switch_ref[:, cols])))
        piece = content_ref[:, cols].astype(F32)
        which = iota(piece.shape, 1) // column
        zero = jnp.zeros_like(piece)
        for h2 in range(2):
            mine = jnp.where(which == h2, piece, 0.0)
            for s2 in range(2):
                base = (h2 * 2 + s2) * width
                row = [mine, zero] if s2 == 0 else [zero, mine]
                value_ref[hp, base : base + width, :] = jnp.concatenate(row, 1).astype(BF16)
        result_ref[hp] = twice(final_ref[:, cols])
    for copy in copies[4:]:
        copy.wait()


def main_kernel(seqs, heads, shifts, *refs):
    blocks = refs[: len(shifts)]
    (
        rows_ref,
        weight_ref,
        gain_ref,
        turned_ref,
        folded_ref,
        gate_ref,
        right_ref,
        value_ref,
        result_ref,
        out_hbm,
        pair_hbm,
        out_ref,
        pair_ref,
        mask_scr,
        rhs_scr,
        logits_scr,
        mixed_scr,
        even_scr,
        odd_scr,
        sems,
        pair_sem,
    ) = refs[len(shifts) :]
    half = seqs // 2
    outer = seqs // 8
    devs = len(shifts)
    _, toks, lanes = blocks[0].shape
    tokens = devs * toks
    tiles = tokens // 128
    spots = positions(devs, toks, shifts)

    def gathered(n):
        return jnp.concatenate([block[n] for block in blocks], axis=0)

    mask = gathered(half)
    own = jnp.where(iota((toks, lanes), 1) < seqs, blocks[0][half], 0)
    inverse = 1.0 / (1.0 + dot_nt(own, mask))
    pick = jnp.where(iota((seqs + 8, lanes), 0) == iota((seqs + 8, lanes), 1), 1.0, 0.0)
    mask_scr[...] = dot_nt(pick.astype(BF16), mask)
    real = mask_scr[seqs : seqs + 1, :]
    factor = rhs_scr.shape[0]
    for so in range(0, outer, 2):
        pieces = []
        for n in (so, so + 1):
            rows = jnp.concatenate([gathered(n * 4 + r) for r in range(4)], axis=1)
            right = dot_nt(right_ref[...], rows).reshape(factor, 8, tokens)
            pieces.append(right * mask_scr[n * 8 : n * 8 + 8, :])
        rhs_scr[:, so * 8 : so * 8 + 16, :] = jnp.concatenate(pieces, axis=1).astype(BF16)
    w_high, w_low = split(weight_ref[...] * gain_ref[...])
    weights = jnp.concatenate([w_high, w_low], axis=0)
    w_sum = jnp.sum(w_high.astype(F32) + w_low.astype(F32), axis=1, keepdims=True)
    channels = turned_ref.shape[1]
    group = even_scr.shape[0] // channels

    def product(g, acc_scr):
        rows = folded_ref[g * group : (g + 1) * group].reshape(group * channels, -1)
        acc_scr[...] = dot(rows, rhs_scr[...].reshape(factor * seqs, tokens))

    def finish(g, acc_scr):
        for n in range(group):
            i = g * group + n
            for jb in range(tiles):
                cols = slice(jb * 128, (jb + 1) * 128)
                update = acc_scr[n * channels : (n + 1) * channels, cols] * inverse[i : i + 1, cols]
                x = (turned_ref[i, :, cols].astype(F32) + update).astype(BF16)
                logits = dot(weights, x)
                x = x.astype(F32)
                turned = x.T.astype(BF16)
                for k in range(128 // toks):
                    spot = spots[jb * (128 // toks) + k]
                    pair_ref[i, pl.ds(spot, toks), :] = turned[k * toks : (k + 1) * toks]
                mean = jnp.mean(x, axis=0, keepdims=True)
                x = x - mean
                scale = lax.rsqrt(jnp.mean(x * x, axis=0, keepdims=True) + 1e-05)
                logits = (logits[:heads] + logits[heads:] - w_sum * mean) * scale
                logits_scr[jb, pl.ds(i, heads, stride=toks), :] = logits
            pltpu.make_async_copy(pair_ref.at[i], pair_hbm.at[i], pair_sem.at[i]).start()

    scratch = (even_scr, odd_scr)
    product(0, even_scr)
    for g in range(toks // group):
        if g + 1 < toks // group:
            product(g + 1, scratch[(g + 1) % 2])
        finish(g, scratch[g % 2])
    logits = jnp.concatenate([logits_scr[jb] for jb in range(tiles)], axis=1)
    logits = jnp.where(real > 0.5, logits, -1000000000.0)
    top = jnp.max(logits, axis=-1, keepdims=True)
    power = jnp.exp(logits - top)
    probs = (power / jnp.sum(power, axis=-1, keepdims=True)).astype(BF16)
    for b in range(0, half, 2):
        mixed = dot(probs, jnp.concatenate([gathered(b), gathered(b + 1)], axis=1)).astype(BF16)
        mixed_scr[b] = mixed[:, :lanes]
        mixed_scr[b + 1] = mixed[:, lanes:]
    total = None
    for hp in range(heads // 2):
        pair = jnp.concatenate(
            [
                mixed_scr[:, (2 * hp + h2) * toks : (2 * hp + h2 + 1) * toks, :].reshape(
                    half * toks, lanes
                )
                for h2 in range(2)
            ],
            axis=1,
        )
        average = dot(pair, value_ref[hp])
        gated = (gate_ref[hp] * average).astype(BF16)
        part = dot_nt(gated, result_ref[hp])
        total = part if total is None else total + part
    width = rows_ref.shape[2]
    total = total.reshape(outer, 4, toks, lanes)
    base = rows_ref[...].astype(F32).reshape(outer, 2, 4, toks, width)
    stores = []
    for so in range(outer):
        for s2 in range(2):
            piece = base[so, s2] + total[so, ..., s2 * width : (s2 + 1) * width]
            out_ref[so * 8 + s2 * 4 : so * 8 + s2 * 4 + 4] = piece.astype(BF16)
        if so % 2:
            here = pl.ds(so // 2 * 16, 16)
            stores.append(
                pltpu.make_async_copy(out_ref.at[here], out_hbm.at[here], sems.at[so // 2])
            )
            stores[-1].start()
    for i in range(toks):
        pltpu.make_async_copy(pair_ref.at[i], pair_hbm.at[i], pair_sem.at[i]).wait()
    for store in stores:
        store.wait()


def far_order(devs):
    far = list(range(4, devs, 4))
    return far[:1] + far[:0:-1]


def shards(
    homolog_embedding,
    pair_state_tiles,
    alignment_mask,
    token_real_mask,
    lineup_standardize_scaling,
    former_factor_proj,
    latter_factor_proj,
    outer_output_weight,
    pair_norm_gain,
    pair_logit_weight,
    content_vector_proj,
    sigmoid_switch_proj,
    final_result_proj,
    *,
    devs,
):
    seqs, toks, width = homolog_embedding.shape
    tokens = devs * toks
    heads = pair_logit_weight.shape[1]
    factor = former_factor_proj.shape[1]
    channels = outer_output_weight.shape[1]
    lanes = 2 * width
    half, outer = seqs // 2, seqs // 8
    params = pltpu.CompilerParams(vmem_limit_bytes=28 << 20)

    def keep(*arrays):
        return [pltpu.with_memory_space_constraint(a, pltpu.HBM) for a in arrays]

    def room(*arrays):
        return [pltpu.VMEM(a.shape, a.dtype) for a in arrays]

    arrays = (
        homolog_embedding,
        alignment_mask.T,
        lineup_standardize_scaling[None],
        token_real_mask[None],
    )
    packed, former = pl.pallas_call(
        pack_kernel,
        out_shape=(
            jax.ShapeDtypeStruct((half + 1, toks, lanes), BF16),
            jax.ShapeDtypeStruct((factor, width), BF16),
        ),
        in_specs=[HB] * 5,
        out_specs=(VM,) * 2,
        scratch_shapes=room(*arrays) + [pltpu.SemaphoreType.DMA((5,))],
        compiler_params=params,
        name="pack",
    )(*keep(*arrays, former_factor_proj.T))

    def swap(block, shift):
        return lax.ppermute(block, "row", [(n, n ^ shift) for n in range(devs)])

    held = {0: packed}
    far = far_order(devs)
    for shift in far:
        held[shift] = swap(packed, shift)
    for bit in (2, 1):
        for shift in list(held):
            held[shift ^ bit] = swap(held[shift], bit)
    shifts = tuple(sorted(held))

    folded, state = pl.pallas_call(
        functools.partial(fold_kernel, seqs),
        out_shape=(
            jax.ShapeDtypeStruct((toks, channels, factor * seqs), BF16),
            jax.ShapeDtypeStruct(pair_state_tiles.shape, BF16),
        ),
        in_specs=[VM] * 2 + [HB] * 2,
        out_specs=(VM,) * 2,
        scratch_shapes=room(outer_output_weight)
        + [
            pltpu.VMEM(outer_output_weight.shape, F32),
            pltpu.VMEM((seqs * toks, 128), F32),
            pltpu.VMEM((factor // 2 * channels, 2 * factor), BF16),
            pltpu.VMEM((toks // 2, 2 * factor, 4 * seqs), BF16),
            pltpu.SemaphoreType.DMA((2,)),
        ],
        compiler_params=params,
        cost_estimate=pl.CostEstimate(flops=10**9, bytes_accessed=10**7, transcendentals=0),
        name="fold",
    )(packed, former, *keep(outer_output_weight, pair_state_tiles))
    arrays = (
        latter_factor_proj.T,
        content_vector_proj,
        sigmoid_switch_proj,
        final_result_proj.T,
    )
    others = (pair_logit_weight.T, pair_norm_gain[None], homolog_embedding)
    gate, right, value, result, *extra = pl.pallas_call(
        functools.partial(gate_kernel, seqs, heads),
        out_shape=(
            jax.ShapeDtypeStruct((heads // 2, half * toks, lanes), F32),
            jax.ShapeDtypeStruct((8 * factor, 8 * width), BF16),
            jax.ShapeDtypeStruct((heads // 2, 4 * width, lanes), BF16),
            jax.ShapeDtypeStruct((heads // 2, lanes, lanes), BF16),
        )
        + tuple(jax.ShapeDtypeStruct(a.shape, a.dtype) for a in others),
        in_specs=[VM] + [HB] * 7,
        out_specs=(VM,) * 7,
        scratch_shapes=room(*arrays) + [pltpu.SemaphoreType.DMA((7,))],
        compiler_params=params,
        cost_estimate=pl.CostEstimate(
            flops=10**8, bytes_accessed=10**6, transcendentals=10**6
        ),
        name="gate",
    )(packed, *keep(*arrays, *others))
    turned = pl.pallas_call(
        functools.partial(turn_kernel, shifts),
        out_shape=jax.ShapeDtypeStruct((toks, channels, tokens), BF16),
        in_specs=[VM],
        out_specs=VM,
        compiler_params=params,
        cost_estimate=pl.CostEstimate(flops=10**7, bytes_accessed=10**6, transcendentals=0),
        name="turn",
    )(state)
    group = GROUP
    out, pair = pl.pallas_call(
        functools.partial(main_kernel, seqs, heads, shifts),
        out_shape=(
            jax.ShapeDtypeStruct(homolog_embedding.shape, BF16),
            jax.ShapeDtypeStruct(pair_state_tiles.shape, BF16),
        ),
        in_specs=[VM] * (devs + 9),
        out_specs=(HB, HB),
        scratch_shapes=room(homolog_embedding)
        + [
            pltpu.VMEM(pair_state_tiles.shape, BF16),
            pltpu.VMEM((seqs + 8, tokens), F32),
            pltpu.VMEM((factor, seqs, tokens), BF16),
            pltpu.VMEM((tokens // 128, heads * toks, 128), F32),
            pltpu.VMEM((half, heads * toks, lanes), BF16),
            pltpu.VMEM((group * channels, tokens), F32),
            pltpu.VMEM((group * channels, tokens), F32),
            pltpu.SemaphoreType.DMA((outer // 2,)),
            pltpu.SemaphoreType.DMA((toks,)),
        ],
        compiler_params=params,
        cost_estimate=pl.CostEstimate(flops=4 * 10**9, bytes_accessed=10**7, transcendentals=10**6),
        name="main",
    )(
        *[held[shift] for shift in shifts],
        extra[2],
        extra[0],
        extra[1],
        turned,
        folded,
        gate,
        right,
        value,
        result,
    )
    return out, pair


def solution(mesh):
    placed = (
        P("groups", "row", None),
        P(("groups", "row"), None, None),
        P("groups", "row"),
        P("groups"),
        P(),
        P(),
        P(),
        P(),
        P(),
        P(),
        P(),
        P(),
        P(),
    )
    devs = mesh.shape["row"]

    def body(*arrays):
        return shards(*arrays, devs=devs)

    return jax.shard_map(
        body,
        mesh=mesh,
        in_specs=placed,
        out_specs=(P("groups", "row", None), P(("groups", "row"), None, None)),
        check_vma=False,
    )
```
